128 devices in a mesh: corpus: 16 (over y, z), blk: 8 (over x, core).
Axes of the slice: x: 4, y: 4, z: 4, core: 2. Of those that a mesh axis runs over, the one named last changes fastest.
Arguments:
- queries: bfloat16 [2048, 32, 128], P(('corpus', 'blk')), may hold values from -0.0625 to 0.0625
- index: bfloat16 [8192, 128, 128], P('corpus'), may hold values from -6 to 6
- cand_owner: int32 [2048, 64, 1], P(('corpus', 'blk')), may hold values from 0 to 15; in each aligned block of 1024 rows (0 to 1023, 1024 to 2047, ..., all dimensions but the last counted through in order) at most 128 rows name the same one
- cand_row: int32 [2048, 64], P(('corpus', 'blk')), may hold values from 0 to 511
- neg_row: int32 [128, 24], P(('corpus', 'blk')), may hold values from 0 to 511
- teacher: float32 [2048, 64], P(('corpus', 'blk')), may hold values from -16 to 16
Outputs:
- losses: float32 [2048], P(('corpus', 'blk'))
- query_grads: float32 [2048, 32, 128], P(('corpus', 'blk'))
The draws below stay inside these ranges and needn't reach their ends.
Inputs may be any that keep to these rules, and one draw needn't show every extreme that they name: `cand_owner`: among the 1024 candidates of one device, no owner shard is named more than 128 times, and some owner shard is named exactly 128 times.
All inputs are finite; a program needn't handle non-finite values.
Results may differ from the reference program's by a relative error of at most 0.007.
Values may be sent and summed in bfloat16 or wider, within the bound.
A program may use at most 256 MiB of HBM per device.

```python
import math
import jax
import jax.numpy as jnp
import numpy as np
from jax import lax

DIM = 128
QT = 32
PT = 128
NCAND = 64
NEG = 24
QDEV = 16
PASS_DEV = 512
NQ = 2048
PASSAGES = 8192
CAP = 128
N_CORPUS = 16
N_BLK = 8
DEVICES = 128


def place_ends(values, rng, least, high):
    longest = values.shape.index(max(values.shape))
    spots = []
    for shift in (0, 1):
        where = [jax.random.randint(jax.random.fold_in(rng, axis), (), 0, length) for axis, length in enumerate(values.shape)]
        where[longest] = (where[longest] + shift) % values.shape[longest]
        spots.append(tuple(where))
    return values.at[spots[0]].set(least).at[spots[1]].set(high)


def shard_levels(key, dims, split, least, high):
    loudness = 1.0
    for dim, shards_of in split:
        steps = jax.random.uniform(jax.random.fold_in(jax.random.fold_in(key, 6), dim), (shards_of,), jnp.float32, least / len(split), high / len(split))
        loudness = loudness * jnp.repeat(jnp.exp(steps), dims[dim] // shards_of).reshape((-1,) + (1,) * (len(dims) - 1 - dim))
    return loudness


def assign_block(rng, own, number, rows, number_of, top, reach, slope):
    ranking = jax.random.permutation(rng, number_of)
    crowded, common = shares(number_of, rows * top, reach, slope, True), shares(number_of, rows * top, reach, slope, False)
    places = jnp.arange(number_of)

    def named(lengths, offset_by):
        used = int((lengths > 0).sum())
        fixed = max(1, used // 4)
        moved = fixed + (places - fixed + offset_by * (used - fixed)) % max(1, number_of - fixed)
        return jnp.zeros((number_of,), jnp.int32).at[ranking[jnp.where(places < fixed, places, moved)]].set(jnp.asarray(lengths, jnp.int32))

    lengths = jnp.where(number % 4 == 0, named(crowded, number // 4), named(common, number - number // 4 - 1))
    mixed = jax.random.permutation(jax.random.fold_in(own, 3), number_of)
    donor, sink = mixed[0:number_of // 2 * 2:2], mixed[1:number_of // 2 * 2:2]
    slack = jnp.minimum(lengths[donor] - 1, reach - lengths[sink]) // 2
    slack = jnp.where((donor == ranking[0]) | (sink == ranking[0]) | (lengths[sink] == 0), 0, jnp.maximum(slack, 0))
    moved = jax.random.randint(jax.random.fold_in(own, 4), (number_of // 2,), 0, 1 << 20) % (slack + 1)
    lengths = lengths.at[donor].add(-moved).at[sink].add(moved)
    items = jnp.searchsorted(jnp.cumsum(lengths), jnp.arange(rows * top), side="right").astype(jnp.int32)
    grid = items.reshape(top, rows).T
    grid = grid[jax.random.permutation(jax.random.fold_in(own, 1), rows)]
    offset_by = jax.random.randint(jax.random.fold_in(own, 2), (rows, 1), 0, top)
    return jnp.take_along_axis(grid, (jnp.arange(top)[None, :] + offset_by) % top, axis=1)


def shares(amount, total, most, skew, full):
    portions = [(1 << 20) // math.isqrt(grade ** skew) + 1 for grade in range(1, amount + 1)]
    largest = most if full else min(most, max(-(-total // amount), total * portions[0] // sum(portions)))
    least = 1 if total - largest >= amount - 1 else 0
    holding, spare = [largest] + [least] * (amount - 1), total - largest - least * (amount - 1)
    while spare > 0:
        free = [i for i in range(1, amount) if holding[i] < largest] or [i for i in range(1, amount) if holding[i] < most]
        pool, left = sum([portions[i] for i in free]), spare
        for i in free:
            more = min(most - holding[i], max(1, left * portions[i] // pool), spare)
            holding[i] = holding[i] + more
            spare = spare - more
    return np.array(holding)


def centred(rng, dims, scale, reach, shards=(), kind=jnp.bfloat16):
    level = shard_levels(rng, dims, shards, -0.22, 0.18) if shards else 1.0
    entries = jax.random.normal(rng, dims, jnp.float32) * scale * level
    return jnp.minimum(jnp.maximum(entries, -reach), reach).astype(kind)


def setup_inputs(seed: int = 0) -> dict:
    arg_keys = jax.random.split(jax.random.key(seed), 7)
    queries = centred(arg_keys[0], (NQ, QT, DIM), 0.01, 0.0625, ((0, 128),))
    index = centred(arg_keys[1], (PASSAGES, PT, DIM), 1.0, 6.0, ((0, 16),))
    cand_owner_keys = jax.random.split(jax.random.fold_in(arg_keys[2], 1), NQ * NCAND // (QDEV * NCAND))
    cand_owner_turns = jax.random.permutation(jax.random.fold_in(arg_keys[2], 3), NQ * NCAND // (QDEV * NCAND))
    cand_owner = jax.vmap(lambda own, number: assign_block(jax.random.fold_in(arg_keys[2], 2), own, number, QDEV * NCAND, N_CORPUS, 1, CAP, 2))(cand_owner_keys, cand_owner_turns).reshape((NQ, NCAND, 1))
    cand_row = place_ends(jax.random.randint(arg_keys[3], (NQ, NCAND), 0, PASS_DEV), jax.random.fold_in(arg_keys[3], 1), 0, PASS_DEV - 1).astype(jnp.int32)
    neg_row = place_ends(jax.random.randint(arg_keys[4], (DEVICES, NEG), 0, PASS_DEV), jax.random.fold_in(arg_keys[4], 1), 0, PASS_DEV - 1).astype(jnp.int32)
    teacher = centred(arg_keys[5], (NQ, NCAND), 3.0, 16.0, ((0, 128),), jnp.float32)
    return dict(queries=queries, index=index, cand_owner=cand_owner, cand_row=cand_row, neg_row=neg_row, teacher=teacher)


inner_temp = 0.1
epsilon = 1e-06

def soft_terms(raw, inverse):
    scaled = raw * inverse
    expo = jnp.exp(scaled / inner_temp)
    totals = lax.optimization_barrier(jnp.sum(expo, axis=-1, keepdims=True))
    score = inner_temp * lax.optimization_barrier(jnp.sum(jnp.log(totals[..., 0]), axis=-1))
    weights = (expo / totals * inverse).astype(jnp.bfloat16)
    return (score, weights)

def tile_inverse(tiles):
    wide = tiles.astype(jnp.float32)
    return lax.rsqrt(lax.optimization_barrier(jnp.sum(wide * wide, axis=-1)) + epsilon)

def one_query(query, tiles, teacher_row):
    widened = query.astype(jnp.float32)
    radius = jnp.sqrt(lax.optimization_barrier(jnp.sum(widened * widened, axis=-1, keepdims=True)) + epsilon)
    unit = widened / radius
    rounded = unit.astype(jnp.bfloat16)
    wide_tiles = tiles.astype(jnp.float32)
    raw = jnp.einsum('id,pjd->pij', rounded.astype(jnp.float32), wide_tiles)
    inverse = tile_inverse(tiles)[:, None, :]
    score, weights = soft_terms(raw, inverse)
    back = jnp.einsum('pij,pjd->pid', weights.astype(jnp.float32), wide_tiles)
    cands = score[:NCAND]
    negs = score[NCAND:]
    total = jnp.sum(jnp.exp(cands)) + jnp.sum(jnp.exp(negs))
    spread = jnp.log(total)
    log_target = teacher_row - jnp.log(jnp.sum(jnp.exp(teacher_row)))
    target = jnp.exp(log_target)
    loss = jnp.sum(target * (log_target - cands + spread))
    grads_score = jnp.concatenate([jnp.exp(cands - spread) - target, jnp.exp(negs - spread)])
    pulled = lax.optimization_barrier(jnp.sum(grads_score[:, None, None] * back, axis=0))
    result = (pulled - unit * lax.optimization_barrier(jnp.sum(unit * pulled, axis=-1, keepdims=True))) / radius
    return (loss, result)

def reference(queries, index, cand_owner, cand_row, neg_row, teacher):
    numbers = jnp.arange(NQ, dtype=jnp.int32)

    def handle(number):
        shard = (number // QDEV // N_BLK).astype(jnp.int32)
        listed = cand_owner[number, :, 0] * PASS_DEV + cand_row[number]
        sampled = lax.dynamic_slice_in_dim(neg_row, (shard * N_BLK).astype(jnp.int32), N_BLK, 0).reshape(-1) + shard * PASS_DEV
        tiles = index[jnp.concatenate([listed, sampled]).astype(jnp.int32)]
        return one_query(queries[number], tiles, teacher[number])
    losses, grads = lax.map(handle, numbers)
    return (losses, grads)
```

```python
import functools
import math

import jax
import jax.numpy as jnp
from jax import lax
from jax.experimental import pallas as pl
from jax.experimental.pallas import tpu as pltpu
from jax.sharding import PartitionSpec as P

MESH = pl.DeviceIdType.MESH
F32, BF16, I32 = jnp.float32, jnp.bfloat16, jnp.int32
EPS = 1e-6
SCALE = 10.0 * math.log2(math.e)
LN2 = math.log(2.0)
ROWS_NT = (((1,), (1,)), ((), ()))


def lane_sum_of_groups(x, group, lane, width):
    shift = group // 2
    while shift:
        x = x + jnp.where(
            (lane & shift) != 0, pltpu.roll(x, shift, 1), pltpu.roll(x, width - shift, 1)
        )
        shift //= 2
    return x


def transpose_pass(first, count, unroll, w_ref, inv_ref, tt_ref):
    def body(b, _):
        rows = [first + b * unroll + u for u in range(unroll)]
        wide = [jnp.transpose(w_ref[r]).astype(F32) for r in rows]
        inv = [lax.rsqrt(jnp.sum(x * x, axis=0, keepdims=True) + EPS) for x in wide]
        for u, r in enumerate(rows):
            inv_ref[pl.ds(r, 1)] = inv[u]
            tt_ref[r] = (wide[u] * (inv[u] * SCALE)).astype(BF16)
        return 0

    lax.fori_loop(0, count // unroll, body, 0)


def negatives(count, unroll, depth, rows_ref, w_ref, qt_ref, acc_ref, sum_ref):
    lane = lax.broadcasted_iota(I32, (1, 128), 1)
    groups = qt_ref.shape[1] // 128
    acc_ref[...] = jnp.zeros_like(acc_ref)
    sum_ref[...] = jnp.zeros_like(sum_ref)

    def body(b, _):
        tiles, flipped = [], []
        for u in range(unroll):
            wide = w_ref[rows_ref[b * unroll + u]].astype(F32)
            square = jnp.sum(wide * wide, axis=-1, keepdims=True)
            tiles.append((wide * (lax.rsqrt(square + EPS) * SCALE)).astype(BF16))
        for u in range(unroll):
            flipped.append(jnp.transpose(tiles[u]))
        items = [(g, u) for g in range(groups) for u in range(unroll)]
        n = len(items)
        sims, factor, expo, back = {}, {}, {}, {}
        total = sums = None
        for step in range(n + 3 * depth):
            i = step
            if i < n:
                g, u = items[i]
                sims[i] = jnp.dot(
                    tiles[u], qt_ref[:, g * 128 : (g + 1) * 128], preferred_element_type=F32
                )
            i = step - depth
            if 0 <= i < n:
                g, u = items[i]
                e = jnp.exp2(sims[i])
                logs = jnp.log2(jnp.sum(e, axis=0, keepdims=True))
                back[i] = jnp.dot(flipped[u], e.astype(BF16), preferred_element_type=F32)
                expo[i] = jnp.exp2(lane_sum_of_groups(logs, 32, lane, 128) * 0.1)
                factor[i] = expo[i] * jnp.exp2(-logs)
            i = step - 3 * depth
            if 0 <= i < n:
                g, u = items[i]
                here = back[i] * factor[i]
                total = here if u == 0 else total + here
                sums = expo[i] if u == 0 else sums + expo[i]
                if u == unroll - 1:
                    acc_ref[:, g * 128 : (g + 1) * 128] += total
                    sum_ref[0:1, g * 128 : (g + 1) * 128] += sums
        return 0

    lax.fori_loop(0, count // unroll, body, 0)


def listed(src, room, unroll, code, targ, keep, w_ref, inv_ref, tt_ref, q_ref, pa, pb, p1, p2):
    zero = jnp.zeros((32, 128), F32)
    one = jnp.zeros((1, 1), F32)

    def body(b, carry):
        acc_a, acc_b, acc_1, acc_2 = carry
        ks = [b * unroll + u for u in range(unroll)]
        cs = [code[src, k] for k in ks]
        sims = [
            jnp.dot(q_ref[c & 15], tt_ref[c >> 4], preferred_element_type=F32) for c in cs
        ]
        expo = [jnp.exp2(x) for x in sims]
        totals = [jnp.sum(x, axis=-1, keepdims=True) for x in expo]
        weights = [(x * inv_ref[pl.ds(c >> 4, 1)]).astype(BF16) for x, c in zip(expo, cs)]
        back = [
            jnp.dot(x, w_ref[c >> 4], preferred_element_type=F32) for x, c in zip(weights, cs)
        ]
        logs = [jnp.log2(x) for x in totals]
        score = [jnp.sum(x, axis=0, keepdims=True) * 0.1 for x in logs]
        top = [jnp.exp2(x) for x in score]
        flat = [jnp.exp2(-x) for x in logs]
        for u, k in enumerate(ks):
            here = back[u] * flat[u]
            stay, target = keep[src, k], targ[src, k]
            acc_a = acc_a * stay + here * top[u]
            acc_b = acc_b * stay + here * target
            acc_1 = acc_1 * stay + top[u]
            acc_2 = acc_2 * stay + score[u] * target
            pa[k] = acc_a
            pb[k] = acc_b
            p1[pl.ds(k, 1)] = jnp.broadcast_to(acc_1, (1, 128))
            p2[pl.ds(k, 1)] = jnp.broadcast_to(acc_2, (1, 128))
        return acc_a, acc_b, acc_1, acc_2

    lax.fori_loop(0, room // unroll, body, (zero, zero, one, one))


def kernel(
    owners, room, chunks,
    code, targ, keep, last, rows, q_ref, index_ref,
    grad_ref, s_ref,
    w, tt, inv, qall, qcur, qt, pa, pb, p1, p2, acc, nsum, back_buf, sum_buf, got, got_sum,
    load_sem, q_send, q_recv, b_send, b_recv, s_send, s_recv,
):
    me = lax.axis_index("corpus")
    count, tokens = qcur.shape[0], qcur.shape[1]

    barrier = pltpu.get_barrier_semaphore()

    def loads(j):
        part = pl.ds(j * (w.shape[0] // chunks), w.shape[0] // chunks)
        return pltpu.make_async_copy(index_ref.at[part], w.at[part], load_sem.at[j])

    def start_load(j, _):
        loads(j).start()
        return 0

    lax.fori_loop(0, chunks, start_load, 0)

    def greet(k, _):
        pl.semaphore_signal(
            barrier, inc=1, device_id={"corpus": lax.rem(me + k, owners)}, device_id_type=MESH
        )
        return 0

    lax.fori_loop(1, owners, greet, 0)

    wide = q_ref[...].astype(F32)
    radius = jnp.sqrt(jnp.sum(wide * wide, axis=-1, keepdims=True) + EPS)
    rounded = (wide / radius).astype(BF16)
    qcur[...] = rounded.reshape(qcur.shape)
    qall[me] = rounded.reshape(qcur.shape)
    qt[...] = jnp.transpose(rounded)

    pl.semaphore_wait(barrier, owners - 1)

    def q_copy(k):
        return pltpu.make_async_remote_copy(
            src_ref=qcur,
            dst_ref=qall.at[me],
            send_sem=q_send.at[k],
            recv_sem=q_recv.at[k],
            device_id={"corpus": lax.rem(me + k, owners)},
            device_id_type=MESH,
        )

    def q_start(k, _):
        q_copy(k).start()
        return 0

    lax.fori_loop(1, owners, q_start, 0)

    part = w.shape[0] // chunks

    def prepare(j, _):
        loads(j).wait()
        transpose_pass(j * part, part, 4, w, inv, tt)
        return 0

    lax.fori_loop(0, chunks, prepare, 0)
    negatives(rows.shape[0], 2, 2, rows, w, qt, acc, nsum)

    def q_sent(k, _):
        q_copy(k).wait_send()
        return 0

    lax.fori_loop(1, owners, q_sent, 0)

    zero = jnp.zeros((32, 128), F32)
    pa[room] = zero
    pb[room] = zero
    p1[room : room + 8] = jnp.zeros((8, 128), F32)
    p2[room : room + 8] = jnp.zeros((8, 128), F32)

    def back_copy(k, src):
        return (
            pltpu.make_async_remote_copy(
                src_ref=back_buf.at[k], dst_ref=got.at[k],
                send_sem=b_send.at[k], recv_sem=b_recv.at[k],
                device_id={"corpus": src}, device_id_type=MESH,
            ),
            pltpu.make_async_remote_copy(
                src_ref=sum_buf.at[k], dst_ref=got_sum.at[k],
                send_sem=s_send.at[k], recv_sem=s_recv.at[k],
                device_id={"corpus": src}, device_id_type=MESH,
            ),
        )

    def source(k, _):
        src = lax.rem(me + owners - k, owners)

        @pl.when(k > 0)
        def _():
            q_copy(k).wait_recv()

        qcur[...] = qall[src]
        listed(src, room, 16, code, targ, keep, w, inv, tt, qcur, pa, pb, p1, p2)

        def extract(q, _):
            at = last[src, q]
            back_buf[k, q, 0:tokens] = pa[at].astype(BF16)
            back_buf[k, q, tokens : 2 * tokens] = pb[at].astype(BF16)
            sum_buf[k, 0, pl.ds(q, 1)] = p1[pl.ds(at, 1)]
            sum_buf[k, 1, pl.ds(q, 1)] = p2[pl.ds(at, 1)]
            return 0

        lax.fori_loop(0, count, extract, 0, unroll=4)

        @pl.when(k > 0)
        def _():
            for copy in back_copy(k, src):
                copy.start()

        return 0

    lax.fori_loop(0, owners, source, 0)

    def take(k, _):
        for copy in back_copy(k, lax.rem(me + owners - k, owners)):
            copy.wait()
        return 0

    lax.fori_loop(1, owners, take, 0)

    sums = sum_buf[0]
    for k in range(1, owners):
        sums = sums + got_sum[k]
    p1[0:count] = sums[0]
    p2[0:count] = sums[1]
    pa_flat = jnp.transpose(acc[...]) * (1.0 / SCALE)
    tn = jnp.transpose(jnp.broadcast_to(nsum[0:1], (128, count * tokens)))
    for q in range(count):
        pa[q] = pa_flat[q * tokens : (q + 1) * tokens]
        pb[q] = tn[q * tokens : (q + 1) * tokens]

    def finish(q, _):
        part_a = pa[q] + back_buf[0, q, 0:tokens].astype(F32)
        part_b = back_buf[0, q, tokens : 2 * tokens].astype(F32)
        for k in range(1, owners):
            part_a = part_a + got[k, q, 0:tokens].astype(F32)
            part_b = part_b + got[k, q, tokens : 2 * tokens].astype(F32)
        whole = pb[q] + p1[pl.ds(q, 1)]
        pulled = part_a / whole - part_b
        own = q_ref[pl.ds(pl.multiple_of(q * tokens, tokens), tokens)].astype(F32)
        rad = jnp.sqrt(jnp.sum(own * own, axis=-1, keepdims=True) + EPS)
        unit = own / rad
        along = jnp.sum(unit * pulled, axis=-1, keepdims=True)
        grad_ref[q] = (pulled - unit * along) / rad
        s_ref[0, pl.ds(q, 1)] = whole[0:1]
        s_ref[1, pl.ds(q, 1)] = p2[pl.ds(q, 1)]
        return 0

    lax.fori_loop(0, count, finish, 0)


def step(queries, index, cand_owner, cand_row, neg_row, teacher):
    count, tokens, dim = queries.shape
    listed_count = cand_row.shape[1]
    owners = lax.axis_size("corpus")
    pairs = count * listed_count
    room = 2 * pairs // owners
    passages = index.shape[0]

    log_target = teacher - jnp.log(jnp.sum(jnp.exp(teacher), axis=1, keepdims=True))
    target = jnp.exp(log_target)

    names = cand_owner.reshape(-1)
    hits = names[:, None] == jnp.arange(owners, dtype=I32)[None, :]
    order = jnp.arange(pairs, dtype=I32)
    before = (order[None, :] < order[:, None]).astype(BF16)
    ranks = jnp.dot(before, hits.astype(BF16), preferred_element_type=F32)
    slots = jnp.sum(jnp.where(hits, ranks, 0.0), axis=1).astype(I32)
    places = names * room + slots
    placer = (places[:, None] == jnp.arange(owners * room, dtype=I32)[None, :]).astype(F32)
    codes = cand_row.reshape(-1) * count + order // listed_count
    values = jnp.stack([codes.astype(F32), target.reshape(-1)], axis=0)
    placed = jnp.dot(
        values, placer, precision=lax.Precision.HIGHEST, preferred_element_type=F32
    ).reshape(2, owners, room)
    number = jnp.sum(hits.reshape(count, listed_count, owners).astype(I32), axis=1).T
    upto = jnp.sum(
        jnp.where(jnp.arange(count)[:, None] <= jnp.arange(count)[None, :], number[:, :, None], 0),
        axis=1,
    )
    ends = jnp.where(number > 0, upto - 1, room).astype(F32)
    ends = jnp.pad(ends, ((0, 0), (0, room - count)))
    message = jnp.concatenate([placed[0], placed[1], ends], axis=1)[:, None, :]
    message = lax.all_to_all(message, "corpus", split_axis=0, concat_axis=0, tiled=True)[:, 0]
    code = message[:, :room].astype(I32)
    targ = message[:, room : 2 * room]
    last = message[:, 2 * room : 2 * room + count].astype(I32)
    whose = code % count
    keep = jnp.concatenate(
        [jnp.zeros((owners, 1), F32), (whose[:, 1:] == whose[:, :-1]).astype(F32)], axis=1
    )
    rows = lax.all_gather(neg_row.reshape(-1), "blk", axis=0, tiled=True)

    smem = pl.BlockSpec(memory_space=pltpu.SMEM)
    vmem = pl.BlockSpec(memory_space=pltpu.VMEM)
    dma = pltpu.SemaphoreType.DMA
    chunks = 16
    grads, sums = pl.pallas_call(
        functools.partial(kernel, owners, room, chunks),
        out_shape=[
            jax.ShapeDtypeStruct((count, tokens, dim), F32),
            jax.ShapeDtypeStruct((2, count, 128), F32),
        ],
        in_specs=[smem] * 5 + [vmem, pl.BlockSpec(memory_space=pl.ANY)],
        out_specs=[vmem, vmem],
        scratch_shapes=[
            pltpu.VMEM(index.shape, BF16),
            pltpu.VMEM((passages, dim, index.shape[1]), BF16),
            pltpu.VMEM((passages, 128), F32),
            pltpu.VMEM((owners, count, tokens, dim), BF16),
            pltpu.VMEM((count, tokens, dim), BF16),
            pltpu.VMEM((dim, count * tokens), BF16),
            pltpu.VMEM((room + 1, tokens, dim), F32),
            pltpu.VMEM((room + 1, tokens, dim), F32),
            pltpu.VMEM((room + 8, 128), F32),
            pltpu.VMEM((room + 8, 128), F32),
            pltpu.VMEM((dim, count * tokens), F32),
            pltpu.VMEM((8, count * tokens), F32),
            pltpu.VMEM((owners, count, 2 * tokens, dim), BF16),
            pltpu.VMEM((owners, 2, count, 128), F32),
            pltpu.VMEM((owners, count, 2 * tokens, dim), BF16),
            pltpu.VMEM((owners, 2, count, 128), F32),
            dma((chunks,)), dma((owners,)), dma((owners,)), dma((owners,)), dma((owners,)),
            dma((owners,)), dma((owners,)),
        ],
        compiler_params=pltpu.CompilerParams(
            collective_id=0, has_side_effects=True, vmem_limit_bytes=58 << 20
        ),
        name="distill",
    )(code, targ, keep, last, rows, queries.reshape(count * tokens, dim), index)

    spread = jnp.log(sums[0, :, 0])
    losses = (
        jnp.sum(target * log_target, axis=1)
        - LN2 * sums[1, :, 0]
        + spread * jnp.sum(target, axis=1)
    )
    return losses, grads


def solution(mesh):
    both = ("corpus", "blk")
    return jax.shard_map(
        step,
        mesh=mesh,
        in_specs=(
            P(both, None, None), P("corpus", None, None), P(both, None, None),
            P(both, None), P(both, None), P(both, None),
        ),
        out_specs=(P(both), P(both, None, None)),
        check_vma=False,
    )
```

```python
import functools
import math

import jax
import jax.numpy as jnp
from jax import lax
from jax.experimental import pallas as pl
from jax.experimental.pallas import tpu as pltpu
from jax.sharding import PartitionSpec as P

MESH = pl.DeviceIdType.MESH
F32, BF16, I32 = jnp.float32, jnp.bfloat16, jnp.int32
EPS = 1e-6
SCALE = 10.0 * math.log2(math.e)
LN2 = math.log(2.0)
ROWS_NT = (((1,), (1,)), ((), ()))


def lane_sum_of_groups(x, group, lane, width):
    shift = group // 2
    while shift:
        x = x + jnp.where(
            (lane & shift) != 0, pltpu.roll(x, shift, 1), pltpu.roll(x, width - shift, 1)
        )
        shift //= 2
    return x


def transpose_pass(first, count, unroll, w_ref, inv_ref, tt_ref):
    def body(b, _):
        rows = [first + b * unroll + u for u in range(unroll)]
        wide = [jnp.transpose(w_ref[r]).astype(F32) for r in rows]
        inv = [lax.rsqrt(jnp.sum(x * x, axis=0, keepdims=True) + EPS) for x in wide]
        for u, r in enumerate(rows):
            inv_ref[pl.ds(r, 1)] = inv[u]
            tt_ref[r] = (wide[u] * (inv[u] * SCALE)).astype(BF16)
        return 0

    lax.fori_loop(0, count // unroll, body, 0)


def build_tables(owners, room, codes_end, names_ref, row_ref, target, turned, place, codes, wants, ends, tab_i, tab_f):
    count, listed = row_ref.shape
    lane = lax.broadcasted_iota(I32, (128, 128), 1)
    line = lax.broadcasted_iota(I32, (128, 128), 0)
    lane_f = lane.astype(F32)
    lower = (lane < line).astype(F32).astype(BF16)

    def flip(x):
        turned[...] = jnp.zeros_like(turned)
        turned[0:count, 0:listed] = x
        return jnp.transpose(turned[...])

    number = lax.broadcasted_iota(I32, row_ref.shape, 0)
    names = flip(names_ref[...].astype(F32))
    code = flip((row_ref[...] * count + number).astype(F32))
    want = flip(target)
    per = 128 // listed
    blocks = count // per
    offset = jnp.zeros((1, 128), F32)
    ends[...] = jnp.zeros_like(ends)
    for r in range(blocks):
        def column(x):
            return jnp.concatenate(
                [x[0:listed, r * per + i : r * per + i + 1] for i in range(per)], axis=0
            )

        hit = (column(names) == lane_f)
        ones = hit.astype(F32)
        rank = jnp.dot(lower, ones.astype(BF16), preferred_element_type=F32) + offset
        where = jnp.sum(jnp.where(hit, rank + lane_f * room, 0.0), axis=1, keepdims=True)
        place[r] = jnp.broadcast_to(where, (128, 128))
        codes[r] = jnp.broadcast_to(column(code), (128, 128))
        wants[r] = jnp.broadcast_to(column(want), (128, 128))
        for i in range(per):
            at = (i + 1) * listed - 1
            upto = rank[at : at + 1] + ones[at : at + 1]
            start = offset if i == 0 else before
            ends[r * per + i : r * per + i + 1] = jnp.where(
                upto > start, jnp.minimum(upto - 1.0, float(room)), float(room)
            )
            before = upto
        offset = before
    turned[...] = jnp.transpose(ends[...])
    tab_i[...] = jnp.zeros_like(tab_i)
    tab_f[...] = jnp.zeros_like(tab_f)
    mark = lax.broadcasted_iota(I32, (1, 128), 1)

    def one_owner(o, _):
        slot = lane_f + (o * room).astype(F32)
        sum_c = jnp.zeros((128, 128), F32)
        sum_w = jnp.zeros((128, 128), F32)
        for r in range(blocks):
            here = place[r] == slot
            sum_c = sum_c + jnp.where(here, codes[r], 0.0)
            sum_w = sum_w + jnp.where(here, wants[r], 0.0)
        c = jnp.clip(jnp.sum(sum_c, axis=0, keepdims=True).astype(I32), 0, codes_end - 1)
        whose = c & (count - 1)
        same = (whose == pltpu.roll(whose, 1, 1)) & (mark > 0)
        tab_i[o, 0:1] = c
        tab_i[o, 1:2] = jnp.clip(turned[pl.ds(o, 1)].astype(I32), 0, room)
        tab_f[o, 0:1] = jnp.sum(sum_w, axis=0, keepdims=True)
        tab_f[o, 1:2] = jnp.where(same, 1.0, 0.0)
        return 0

    lax.fori_loop(0, owners, one_owner, 0)


def negatives(unroll, rows_ref, holders, each, tt_ref, qt_ref, acc_ref, sum_ref):
    width = qt_ref.shape[1]
    lane = lax.broadcasted_iota(I32, (1, width), 1)
    acc_ref[...] = jnp.zeros_like(acc_ref)
    sum_ref[...] = jnp.zeros_like(sum_ref)
    steps = each // unroll

    def body(b, _):
        holder, first = b // steps, lax.rem(b, steps) * unroll
        flipped = [tt_ref[rows_ref[holder, 0, first + u]] for u in range(unroll)]
        tiles = jnp.concatenate([jnp.transpose(t) for t in flipped], axis=0)
        sims = jnp.dot(tiles, qt_ref[...], preferred_element_type=F32)
        expo = jnp.exp2(sims)
        parts = [expo[u * 128 : (u + 1) * 128] for u in range(unroll)]
        logs = jnp.log2(
            jnp.concatenate([jnp.sum(x, axis=0, keepdims=True) for x in parts], axis=0)
        )
        top = jnp.exp2(lane_sum_of_groups(logs, 32, lane, width) * 0.1)
        factor = top * jnp.exp2(-logs)
        weights = jnp.concatenate(
            [(parts[u] * factor[u : u + 1]).astype(BF16) for u in range(unroll)], axis=0
        )
        acc_ref[...] += jnp.dot(
            jnp.concatenate(flipped, axis=1), weights, preferred_element_type=F32
        )
        sum_ref[0:1] += jnp.sum(top, axis=0, keepdims=True)
        return 0

    lax.fori_loop(0, holders * steps, body, 0)


def paired_dots(left, right):
    zero = jnp.zeros(left[0].shape, left[0].dtype)
    m = left[0].shape[0]
    out = []
    for i in range(0, len(left), 2):
        both = jnp.concatenate(
            [
                jnp.concatenate([left[i], zero], axis=1),
                jnp.concatenate([zero, left[i + 1]], axis=1),
            ],
            axis=0,
        )
        stacked = jnp.concatenate([right[i], right[i + 1]], axis=0)
        two = jnp.dot(both, stacked, preferred_element_type=F32)
        out += [two[:m], two[m:]]
    return out


def listed_pairs(src, room, unroll, tab_i, tab_f, w_ref, inv_ref, tt_ref, q_ref, pa, pb, p1, p2):
    zero = jnp.zeros((32, 128), F32)
    one = jnp.zeros((1, 1), F32)

    def body(b, carry):
        acc_a, acc_b, acc_1, acc_2 = carry
        ks = [b * unroll + u for u in range(unroll)]
        cs = [tab_i[src, 0, k] for k in ks]
        sims = paired_dots([q_ref[c & 15] for c in cs], [tt_ref[c >> 4] for c in cs])
        expo = [jnp.exp2(x) for x in sims]
        totals = [jnp.sum(x, axis=-1, keepdims=True) for x in expo]
        weights = [(x * inv_ref[pl.ds(c >> 4, 1)]).astype(BF16) for x, c in zip(expo, cs)]
        back = paired_dots(weights, [w_ref[c >> 4] for c in cs])
        logs = [jnp.log2(x) for x in totals]
        score = [jnp.sum(x, axis=0, keepdims=True) * 0.1 for x in logs]
        top = [jnp.exp2(x) for x in score]
        flat = [jnp.exp2(-x) for x in logs]
        for u, k in enumerate(ks):
            here = back[u] * flat[u]
            target, stay = tab_f[src, 0, k], tab_f[src, 1, k]
            acc_a = acc_a * stay + here * top[u]
            acc_b = acc_b * stay + here * target
            acc_1 = acc_1 * stay + top[u]
            acc_2 = acc_2 * stay + score[u] * target
            pa[k] = acc_a.astype(BF16)
            pb[k] = acc_b.astype(BF16)
            p1[pl.ds(k, 1)] = jnp.broadcast_to(acc_1, (1, 128))
            p2[pl.ds(k, 1)] = jnp.broadcast_to(acc_2, (1, 128))
        return acc_a, acc_b, acc_1, acc_2

    lax.fori_loop(0, room // unroll, body, (zero, zero, one, one))


def kernel(
    owners, holders, room, chunks, sampled,
    names_ref, row_ref, neg_ref, teacher_ref, q_ref, index_ref,
    grad_ref, loss_ref,
    w, tt, inv, qall, qcur, qt, pa, pb, p1, p2, acc, nsum, flat_a, flat_s, stats,
    turned, ends, place, codes, wants, tab_i, tab_f, all_i, all_f, all_n,
    back_buf, sum_buf, got, got_sum,
    code_s, mark_s, rows_s,
    load_sem, q_send, q_recv, i_send, i_recv, f_send, f_recv, n_send, n_recv,
    b_send, b_recv, s_send, s_recv, smem_sem,
):
    me = lax.axis_index("corpus")
    seat = lax.axis_index("blk")
    count, tokens = qcur.shape[0], qcur.shape[1]
    part = w.shape[0] // chunks
    barrier = pltpu.get_barrier_semaphore()

    def each(first, last, act):
        def body(k, _):
            act(k)
            return 0

        lax.fori_loop(first, last, body, 0)

    def loads(j):
        rows = pl.ds(j * part, part)
        return pltpu.make_async_copy(index_ref.at[rows], w.at[rows], load_sem.at[j])

    def owner(k):
        return {"corpus": lax.rem(me + k, owners)}

    def holder(k):
        return {"blk": lax.rem(seat + k, holders)}

    def remote(src, dst, send, recv, k, device):
        return pltpu.make_async_remote_copy(
            src_ref=src, dst_ref=dst, send_sem=send.at[k], recv_sem=recv.at[k],
            device_id=device, device_id_type=MESH,
        )

    def greet(device):
        pl.semaphore_signal(barrier, inc=1, device_id=device, device_id_type=MESH)

    each(0, chunks, lambda j: loads(j).start())
    each(1, owners, lambda k: greet(owner(k)))
    each(1, holders, lambda k: greet(holder(k)))

    wide = q_ref[...].astype(F32)
    radius = jnp.sqrt(jnp.sum(wide * wide, axis=-1, keepdims=True) + EPS)
    rounded = (wide / radius).astype(BF16)
    qcur[...] = rounded.reshape(qcur.shape)
    qall[me] = rounded.reshape(qcur.shape)
    qt[...] = jnp.transpose(rounded)
    all_n[seat] = neg_ref[...]

    pl.semaphore_wait(barrier, owners + holders - 2)

    def n_copy(k):
        return remote(neg_ref, all_n.at[seat], n_send, n_recv, k, holder(k))

    def q_copy(k):
        return remote(qcur, qall.at[me], q_send, q_recv, k, owner(k))

    def table_copies(k):
        to = lax.rem(me + k, owners)
        return (
            remote(tab_i.at[to], all_i.at[me], i_send, i_recv, k, owner(k)),
            remote(tab_f.at[to], all_f.at[me], f_send, f_recv, k, owner(k)),
        )

    each(1, holders, lambda k: n_copy(k).start())
    each(1, owners, lambda k: q_copy(k).start())

    teacher = teacher_ref[...]
    log_target = teacher - jnp.log(jnp.sum(jnp.exp(teacher), axis=1, keepdims=True))
    target = jnp.exp(log_target)
    stats[0] = jnp.broadcast_to(jnp.sum(target * log_target, axis=1, keepdims=True), (count, 128))
    stats[1] = jnp.broadcast_to(jnp.sum(target, axis=1, keepdims=True), (count, 128))
    build_tables(
        owners, room, w.shape[0] * count, names_ref, row_ref, target, turned, place, codes, wants, ends, tab_i, tab_f
    )
    all_i[me] = tab_i[me]
    all_f[me] = tab_f[me]
    each(1, owners, lambda k: [copy.start() for copy in table_copies(k)])

    def prepare(j):
        loads(j).wait()
        transpose_pass(j * part, part, 8, w, inv, tt)

    each(0, chunks, prepare)
    each(1, holders, lambda k: n_copy(k).wait())
    each(1, owners, lambda k: [copy.wait() for copy in table_copies(k)])
    moves = [
        pltpu.make_async_copy(all_n, rows_s, smem_sem.at[0]),
        pltpu.make_async_copy(all_i, code_s, smem_sem.at[1]),
        pltpu.make_async_copy(all_f, mark_s, smem_sem.at[2]),
    ]
    for move in moves:
        move.start()
    for move in moves:
        move.wait()
    negatives(8, rows_s, holders, sampled, tt, qt, acc, nsum)
    each(1, owners, lambda k: q_copy(k).wait_send())

    pa[room] = jnp.zeros((tokens, 128), BF16)
    pb[room] = jnp.zeros((tokens, 128), BF16)
    p1[room : room + 8] = jnp.zeros((8, 128), F32)
    p2[room : room + 8] = jnp.zeros((8, 128), F32)

    def back_copies(k):
        to = {"corpus": lax.rem(me + owners - k, owners)}
        return (
            remote(back_buf.at[k], got.at[k], b_send, b_recv, k, to),
            remote(sum_buf.at[k], got_sum.at[k], s_send, s_recv, k, to),
        )

    def source(k):
        src = lax.rem(me + owners - k, owners)

        @pl.when(k > 0)
        def _():
            q_copy(k).wait_recv()

        qcur[...] = qall[src]
        listed_pairs(src, room, 32, code_s, mark_s, w, inv, tt, qcur, pa, pb, p1, p2)

        def extract(q, _):
            at = code_s[src, 1, q]
            back_buf[k, q, 0:tokens] = pa[at]
            back_buf[k, q, tokens : 2 * tokens] = pb[at]
            sum_buf[k, 0, pl.ds(q, 1)] = p1[pl.ds(at, 1)]
            sum_buf[k, 1, pl.ds(q, 1)] = p2[pl.ds(at, 1)]
            return 0

        lax.fori_loop(0, count, extract, 0, unroll=4)

        @pl.when(k > 0)
        def _():
            for copy in back_copies(k):
                copy.start()

    each(0, owners, source)

    turned_a = jnp.transpose(acc[...]) * (1.0 / SCALE)
    turned_s = jnp.transpose(jnp.broadcast_to(nsum[0:1], (128, count * tokens)))
    flat_a[...] = turned_a.reshape(flat_a.shape)
    flat_s[...] = turned_s.reshape(flat_s.shape)

    each(1, owners, lambda k: [copy.wait() for copy in back_copies(k)])
    sums = sum_buf[0]
    for k in range(1, owners):
        sums = sums + got_sum[k]
    p1[0:count] = sums[0]
    p2[0:count] = sums[1]

    def finish(q, _):
        part_a = flat_a[q] + back_buf[0, q, 0:tokens].astype(F32)
        part_b = back_buf[0, q, tokens : 2 * tokens].astype(F32)
        for k in range(1, owners):
            part_a = part_a + got[k, q, 0:tokens].astype(F32)
            part_b = part_b + got[k, q, tokens : 2 * tokens].astype(F32)
        whole = flat_s[q] + p1[pl.ds(q, 1)]
        pulled = part_a / whole - part_b
        own = q_ref[pl.ds(pl.multiple_of(q * tokens, tokens), tokens)].astype(F32)
        rad = jnp.sqrt(jnp.sum(own * own, axis=-1, keepdims=True) + EPS)
        unit = own / rad
        along = jnp.sum(unit * pulled, axis=-1, keepdims=True)
        grad_ref[q] = (pulled - unit * along) / rad
        one = pl.ds(q, 1)
        loss_ref[one] = stats[0, one] - LN2 * p2[one] + jnp.log(whole[0:1]) * stats[1, one]
        return 0

    lax.fori_loop(0, count, finish, 0, unroll=2)


def step(queries, index, cand_owner, cand_row, neg_row, teacher):
    count, tokens, dim = queries.shape
    listed = cand_row.shape[1]
    owners, holders = lax.axis_size("corpus"), lax.axis_size("blk")
    room = 2 * count * listed // owners
    passages = index.shape[0]
    width = count * tokens
    negs = jnp.pad(neg_row, ((0, 7), (0, 128 - neg_row.shape[1])))

    smem = pltpu.SMEM
    vmem = pl.BlockSpec(memory_space=pltpu.VMEM)
    dma = pltpu.SemaphoreType.DMA
    chunks = 16
    grads, losses = pl.pallas_call(
        functools.partial(kernel, owners, holders, room, chunks, neg_row.shape[1]),
        out_shape=[
            jax.ShapeDtypeStruct((count, tokens, dim), F32),
            jax.ShapeDtypeStruct((count, 128), F32),
        ],
        in_specs=[vmem] * 5 + [pl.BlockSpec(memory_space=pl.ANY)],
        out_specs=[vmem, vmem],
        scratch_shapes=[
            pltpu.VMEM(index.shape, BF16),
            pltpu.VMEM((passages, dim, index.shape[1]), BF16),
            pltpu.VMEM((passages, 128), F32),
            pltpu.VMEM((owners, count, tokens, dim), BF16),
            pltpu.VMEM((count, tokens, dim), BF16),
            pltpu.VMEM((dim, width), BF16),
            pltpu.VMEM((room + 1, tokens, dim), BF16),
            pltpu.VMEM((room + 1, tokens, dim), BF16),
            pltpu.VMEM((room + 8, 128), F32),
            pltpu.VMEM((room + 8, 128), F32),
            pltpu.VMEM((dim, width), F32),
            pltpu.VMEM((8, width), F32),
            pltpu.VMEM((count, tokens, dim), F32),
            pltpu.VMEM((count, tokens, dim), F32),
            pltpu.VMEM((2, count, 128), F32),
            pltpu.VMEM((128, 128), F32),
            pltpu.VMEM((128, 128), F32),
            pltpu.VMEM((count * listed // 128, 128, 128), F32),
            pltpu.VMEM((count * listed // 128, 128, 128), F32),
            pltpu.VMEM((count * listed // 128, 128, 128), F32),
            pltpu.VMEM((owners, 8, 128), I32),
            pltpu.VMEM((owners, 8, 128), F32),
            pltpu.VMEM((owners, 8, 128), I32),
            pltpu.VMEM((owners, 8, 128), F32),
            pltpu.VMEM((holders, 8, 128), I32),
            pltpu.VMEM((owners, count, 2 * tokens, dim), BF16),
            pltpu.VMEM((owners, 2, count, 128), F32),
            pltpu.VMEM((owners, count, 2 * tokens, dim), BF16),
            pltpu.VMEM((owners, 2, count, 128), F32),
            smem((owners, 8, 128), I32),
            smem((owners, 8, 128), F32),
            smem((holders, 8, 128), I32),
            dma((chunks,)),
            *[dma((owners,)) for _ in range(6)],
            *[dma((holders,)) for _ in range(2)],
            *[dma((owners,)) for _ in range(4)],
            dma((3,)),
        ],
        compiler_params=pltpu.CompilerParams(
            collective_id=0, has_side_effects=True, vmem_limit_bytes=60 << 20
        ),
        name="distill",
    )(
        cand_owner.reshape(count, listed), cand_row, negs, teacher,
        queries.reshape(width, dim), index,
    )
    return losses[:, 0], grads


def solution(mesh):
    both = ("corpus", "blk")
    return jax.shard_map(
        step,
        mesh=mesh,
        in_specs=(
            P(both, None, None), P("corpus", None, None), P(both, None, None),
            P(both, None), P(both, None), P(both, None),
        ),
        out_specs=(P(both), P(both, None, None)),
        check_vma=False,
    )
```

```python
import functools
import math

import jax
import jax.numpy as jnp
from jax import lax
from jax.experimental import pallas as pl
from jax.experimental.pallas import tpu as pltpu
from jax.sharding import PartitionSpec as P

MESH = pl.DeviceIdType.MESH
F32, BF16, I32 = jnp.float32, jnp.bfloat16, jnp.int32
EPS = 1e-6
SCALE = 10.0 * math.log2(math.e)
LN2 = math.log(2.0)
ROWS_NT = (((1,), (1,)), ((), ()))


def lane_sum_of_groups(x, group, lane, width):
    shift = group // 2
    while shift:
        x = x + jnp.where(
            (lane & shift) != 0, pltpu.roll(x, shift, 1), pltpu.roll(x, width - shift, 1)
        )
        shift //= 2
    return x


def transpose_pass(first, count, unroll, w_ref, inv_ref, tt_ref):
    def body(b, _):
        rows = [first + b * unroll + u for u in range(unroll)]
        wide = [jnp.transpose(w_ref[r]).astype(F32) for r in rows]
        inv = [lax.rsqrt(jnp.sum(x * x, axis=0, keepdims=True) + EPS) for x in wide]
        for u, r in enumerate(rows):
            inv_ref[pl.ds(r, 1)] = inv[u]
            tt_ref[r] = (wide[u] * (inv[u] * SCALE)).astype(BF16)
        return 0

    lax.fori_loop(0, count // unroll, body, 0)


def build_tables(owners, room, codes_end, names_ref, row_ref, target, turned, place, codes, wants, ends, tab_i, tab_f):
    count, listed = row_ref.shape
    lane = lax.broadcasted_iota(I32, (128, 128), 1)
    line = lax.broadcasted_iota(I32, (128, 128), 0)
    lane_f = lane.astype(F32)
    lower = (lane < line).astype(F32).astype(BF16)

    def flip(x):
        turned[...] = jnp.zeros_like(turned)
        turned[0:count, 0:listed] = x
        return jnp.transpose(turned[...])

    number = lax.broadcasted_iota(I32, row_ref.shape, 0)
    names = flip(names_ref[...].astype(F32))
    code = flip((row_ref[...] * count + number).astype(F32))
    want = flip(target)
    per = 128 // listed
    blocks = count // per
    offset = jnp.zeros((1, 128), F32)
    ends[...] = jnp.zeros_like(ends)
    for r in range(blocks):
        def column(x):
            return jnp.concatenate(
                [x[0:listed, r * per + i : r * per + i + 1] for i in range(per)], axis=0
            )

        hit = (column(names) == lane_f)
        ones = hit.astype(F32)
        rank = jnp.dot(lower, ones.astype(BF16), preferred_element_type=F32) + offset
        where = jnp.sum(jnp.where(hit, rank + lane_f * room, 0.0), axis=1, keepdims=True)
        place[r] = jnp.broadcast_to(where, (128, 128))
        codes[r] = jnp.broadcast_to(column(code), (128, 128))
        wants[r] = jnp.broadcast_to(column(want), (128, 128))
        for i in range(per):
            at = (i + 1) * listed - 1
            upto = rank[at : at + 1] + ones[at : at + 1]
            start = offset if i == 0 else before
            ends[r * per + i : r * per + i + 1] = jnp.where(
                upto > start, jnp.minimum(upto - 1.0, float(room)), float(room)
            )
            before = upto
        offset = before
    turned[...] = jnp.transpose(ends[...])
    tab_i[...] = jnp.zeros_like(tab_i)
    tab_f[...] = jnp.zeros_like(tab_f)
    mark = lax.broadcasted_iota(I32, (1, 128), 1)

    def one_owner(o, _):
        slot = lane_f + (o * room).astype(F32)
        sum_c = jnp.zeros((128, 128), F32)
        sum_w = jnp.zeros((128, 128), F32)
        for r in range(blocks):
            here = place[r] == slot
            sum_c = sum_c + jnp.where(here, codes[r], 0.0)
            sum_w = sum_w + jnp.where(here, wants[r], 0.0)
        c = jnp.clip(jnp.sum(sum_c, axis=0, keepdims=True).astype(I32), 0, codes_end - 1)
        whose = c & (count - 1)
        same = (whose == pltpu.roll(whose, 1, 1)) & (mark > 0)
        tab_i[o, 0:1] = c
        tab_i[o, 1:2] = jnp.clip(turned[pl.ds(o, 1)].astype(I32), 0, room)
        tab_f[o, 0:1] = jnp.sum(sum_w, axis=0, keepdims=True)
        tab_f[o, 1:2] = jnp.where(same, 1.0, 0.0)
        return 0

    lax.fori_loop(0, owners, one_owner, 0)


def negatives(first_step, last_step, unroll, rows_ref, each, tt_ref, qt_ref, acc_ref, sum_ref):
    width = qt_ref.shape[1]
    lane = lax.broadcasted_iota(I32, (1, width), 1)
    steps = each // unroll

    def body(b, _):
        holder, first = b // steps, lax.rem(b, steps) * unroll
        flipped = [tt_ref[rows_ref[holder, 0, first + u]] for u in range(unroll)]
        tiles = jnp.concatenate([jnp.transpose(t) for t in flipped], axis=0)
        sims = jnp.dot(tiles, qt_ref[...], preferred_element_type=F32)
        expo = jnp.exp2(sims)
        parts = [expo[u * 128 : (u + 1) * 128] for u in range(unroll)]
        logs = jnp.log2(
            jnp.concatenate([jnp.sum(x, axis=0, keepdims=True) for x in parts], axis=0)
        )
        top = jnp.exp2(lane_sum_of_groups(logs, 32, lane, width) * 0.1)
        factor = top * jnp.exp2(-logs)
        weights = jnp.concatenate(
            [(parts[u] * factor[u : u + 1]).astype(BF16) for u in range(unroll)], axis=0
        )
        acc_ref[...] += jnp.dot(
            jnp.concatenate(flipped, axis=1), weights, preferred_element_type=F32
        )
        sum_ref[0:1] += jnp.sum(top, axis=0, keepdims=True)
        return 0

    lax.fori_loop(first_step, last_step, body, 0)


def paired_dots(left, right):
    zero = jnp.zeros(left[0].shape, left[0].dtype)
    m = left[0].shape[0]
    out = []
    for i in range(0, len(left), 2):
        both = jnp.concatenate(
            [
                jnp.concatenate([left[i], zero], axis=1),
                jnp.concatenate([zero, left[i + 1]], axis=1),
            ],
            axis=0,
        )
        stacked = jnp.concatenate([right[i], right[i + 1]], axis=0)
        two = jnp.dot(both, stacked, preferred_element_type=F32)
        out += [two[:m], two[m:]]
    return out


def listed_pairs(src, room, unroll, tab_i, tab_f, w_ref, inv_ref, tt_ref, q_ref, pa, pb, p1, p2):
    zero = jnp.zeros((32, 128), F32)
    one = jnp.zeros((1, 1), F32)

    def body(b, carry):
        acc_a, acc_b, acc_1, acc_2 = carry
        ks = [b * unroll + u for u in range(unroll)]
        cs = [tab_i[src, 0, k] for k in ks]
        sims = paired_dots([q_ref[c & 15] for c in cs], [tt_ref[c >> 4] for c in cs])
        expo = [jnp.exp2(x) for x in sims]
        totals = [jnp.sum(x, axis=-1, keepdims=True) for x in expo]
        weights = [(x * inv_ref[pl.ds(c >> 4, 1)]).astype(BF16) for x, c in zip(expo, cs)]
        back = paired_dots(weights, [w_ref[c >> 4] for c in cs])
        logs = [jnp.log2(x) for x in totals]
        score = [jnp.sum(x, axis=0, keepdims=True) * 0.1 for x in logs]
        top = [jnp.exp2(x) for x in score]
        flat = [jnp.exp2(-x) for x in logs]
        for u, k in enumerate(ks):
            here = back[u] * flat[u]
            target, stay = tab_f[src, 0, k], tab_f[src, 1, k]
            acc_a = acc_a * stay + here * top[u]
            acc_b = acc_b * stay + here * target
            acc_1 = acc_1 * stay + top[u]
            acc_2 = acc_2 * stay + score[u] * target
            pa[k] = acc_a.astype(BF16)
            pb[k] = acc_b.astype(BF16)
            p1[pl.ds(k, 1)] = jnp.broadcast_to(acc_1, (1, 128))
            p2[pl.ds(k, 1)] = jnp.broadcast_to(acc_2, (1, 128))
        return acc_a, acc_b, acc_1, acc_2

    lax.fori_loop(0, room // unroll, body, (zero, zero, one, one))


def kernel(
    owners, holders, room, chunks, sampled,
    names_ref, row_ref, neg_ref, teacher_ref, q_ref, index_ref,
    grad_ref, loss_ref,
    w, tt, inv, qall, qcur, qt, pa, pb, p1, p2, acc, nsum, flat_a, flat_s, stats,
    turned, ends, place, codes, wants, tab_i, tab_f, all_i, all_f, all_n, neg_own,
    back_buf, sum_buf, got, got_sum,
    code_s, mark_s, rows_s,
    load_sem, q_send, q_recv, i_send, i_recv, f_send, f_recv, n_send, n_recv,
    b_send, b_recv, s_send, s_recv, smem_sem,
):
    me = lax.axis_index("corpus")
    seat = lax.axis_index("blk")
    count, tokens = qcur.shape[0], qcur.shape[1]
    part = w.shape[0] // chunks
    barrier = pltpu.get_barrier_semaphore()

    def each(first, last, act):
        def body(k, _):
            act(k)
            return 0

        lax.fori_loop(first, last, body, 0)

    def loads(j):
        rows = pl.ds(j * part, part)
        return pltpu.make_async_copy(index_ref.at[rows], w.at[rows], load_sem.at[j])

    side = math.isqrt(owners)
    own = owners // 2

    def shifted(m, sign):
        dy = side // 2 + m // side
        dz = dy + lax.rem(m, side)
        y = lax.rem(me // side + sign * lax.rem(dy, side) + side, side)
        z = lax.rem(lax.rem(me, side) + sign * lax.rem(dz, side) + side, side)
        return y * side + z

    def owner(m):
        return {"corpus": shifted(m, 1)}

    def peers(act):
        each(0, own, act)
        each(own + 1, owners, act)

    def holder(k):
        return {"blk": lax.rem(seat + k, holders)}

    def remote(src, dst, send, recv, k, device):
        return pltpu.make_async_remote_copy(
            src_ref=src, dst_ref=dst, send_sem=send.at[k], recv_sem=recv.at[k],
            device_id=device, device_id_type=MESH,
        )

    def greet(device):
        pl.semaphore_signal(barrier, inc=1, device_id=device, device_id_type=MESH)

    each(0, chunks, lambda j: loads(j).start())
    peers(lambda k: greet(owner(k)))
    each(1, holders, lambda k: greet(holder(k)))

    wide = q_ref[...].astype(F32)
    radius = jnp.sqrt(jnp.sum(wide * wide, axis=-1, keepdims=True) + EPS)
    rounded = (wide / radius).astype(BF16)
    qcur[...] = rounded.reshape(qcur.shape)
    qall[me] = rounded.reshape(qcur.shape)
    qt[...] = jnp.transpose(rounded)
    neg_own[...] = jnp.zeros_like(neg_own)
    neg_own[0:1, 0:sampled] = neg_ref[...]
    all_n[seat] = neg_own[...]

    pl.semaphore_wait(barrier, owners + holders - 2)

    def n_copy(k):
        return remote(neg_own, all_n.at[seat], n_send, n_recv, k, holder(k))

    def q_copy(k):
        return remote(qcur, qall.at[me], q_send, q_recv, k, owner(k))

    def table_copies(k):
        to = shifted(k, 1)
        return (
            remote(tab_i.at[to], all_i.at[me], i_send, i_recv, k, owner(k)),
            remote(tab_f.at[to], all_f.at[me], f_send, f_recv, k, owner(k)),
        )

    each(1, holders, lambda k: n_copy(k).start())
    peers(lambda k: q_copy(k).start())

    teacher = teacher_ref[...]
    log_target = teacher - jnp.log(jnp.sum(jnp.exp(teacher), axis=1, keepdims=True))
    target = jnp.exp(log_target)
    stats[0] = jnp.broadcast_to(jnp.sum(target * log_target, axis=1, keepdims=True), (count, 128))
    stats[1] = jnp.broadcast_to(jnp.sum(target, axis=1, keepdims=True), (count, 128))
    build_tables(
        owners, room, w.shape[0] * count, names_ref, row_ref, target, turned, place, codes, wants, ends, tab_i, tab_f
    )
    all_i[me] = tab_i[me]
    all_f[me] = tab_f[me]
    peers(lambda k: [copy.start() for copy in table_copies(k)])

    def prepare(j):
        loads(j).wait()
        transpose_pass(j * part, part, 8, w, inv, tt)

    each(0, chunks, prepare)
    each(1, holders, lambda k: n_copy(k).wait())
    peers(lambda k: [copy.wait() for copy in table_copies(k)])
    moves = [
        pltpu.make_async_copy(all_n, rows_s, smem_sem.at[0]),
        pltpu.make_async_copy(all_i, code_s, smem_sem.at[1]),
        pltpu.make_async_copy(all_f, mark_s, smem_sem.at[2]),
    ]
    for move in moves:
        move.start()
    for move in moves:
        move.wait()
    acc[...] = jnp.zeros_like(acc)
    nsum[...] = jnp.zeros_like(nsum)
    neg_steps = holders * sampled // 8
    early = neg_steps // 3
    negatives(0, early, 8, rows_s, sampled, tt, qt, acc, nsum)
    peers(lambda k: q_copy(k).wait_send())

    pa[room] = jnp.zeros((tokens, 128), BF16)
    pb[room] = jnp.zeros((tokens, 128), BF16)
    p1[room : room + 8] = jnp.zeros((8, 128), F32)
    p2[room : room + 8] = jnp.zeros((8, 128), F32)

    def back_copies(k):
        to = {"corpus": shifted(k, -1)}
        return (
            remote(back_buf.at[k], got.at[k], b_send, b_recv, k, to),
            remote(sum_buf.at[k], got_sum.at[k], s_send, s_recv, k, to),
        )

    def source(k):
        src = shifted(k, -1)

        @pl.when(k != own)
        def _():
            q_copy(k).wait_recv()

        qcur[...] = qall[src]
        listed_pairs(src, room, 32, code_s, mark_s, w, inv, tt, qcur, pa, pb, p1, p2)

        def extract(q, _):
            at = code_s[src, 1, q]
            back_buf[k, q, 0:tokens] = pa[at]
            back_buf[k, q, tokens : 2 * tokens] = pb[at]
            sum_buf[k, 0, pl.ds(q, 1)] = p1[pl.ds(at, 1)]
            sum_buf[k, 1, pl.ds(q, 1)] = p2[pl.ds(at, 1)]
            return 0

        lax.fori_loop(0, count, extract, 0, unroll=4)

        @pl.when(k != own)
        def _():
            for copy in back_copies(k):
                copy.start()

    each(0, owners, source)
    negatives(early, neg_steps, 8, rows_s, sampled, tt, qt, acc, nsum)

    turned_a = jnp.transpose(acc[...]) * (1.0 / SCALE)
    turned_s = jnp.transpose(jnp.broadcast_to(nsum[0:1], (128, count * tokens)))
    flat_a[...] = turned_a.reshape(flat_a.shape)
    flat_s[...] = turned_s.reshape(flat_s.shape)

    peers(lambda k: [copy.wait() for copy in back_copies(k)])
    sums = sum_buf[own]
    others = [k for k in range(owners) if k != own]
    for k in others:
        sums = sums + got_sum[k]
    p1[0:count] = sums[0]
    p2[0:count] = sums[1]

    def finish(q, _):
        part_a = flat_a[q] + back_buf[own, q, 0:tokens].astype(F32)
        part_b = back_buf[own, q, tokens : 2 * tokens].astype(F32)
        for k in others:
            part_a = part_a + got[k, q, 0:tokens].astype(F32)
            part_b = part_b + got[k, q, tokens : 2 * tokens].astype(F32)
        whole = flat_s[q] + p1[pl.ds(q, 1)]
        pulled = part_a / whole - part_b
        raw = q_ref[pl.ds(pl.multiple_of(q * tokens, tokens), tokens)].astype(F32)
        rad = jnp.sqrt(jnp.sum(raw * raw, axis=-1, keepdims=True) + EPS)
        unit = raw / rad
        along = jnp.sum(unit * pulled, axis=-1, keepdims=True)
        grad_ref[q] = (pulled - unit * along) / rad
        one = pl.ds(q, 1)
        stats[2, one] = stats[0, one] - LN2 * p2[one] + jnp.log(whole[0:1]) * stats[1, one]
        return 0

    lax.fori_loop(0, count, finish, 0, unroll=2)
    turned[...] = jnp.zeros_like(turned)
    turned[0:count] = stats[2]
    loss_ref[...] = jnp.transpose(turned[...])[0:1, 0:count]


def step(queries, index, cand_owner, cand_row, neg_row, teacher):
    count, tokens, dim = queries.shape
    listed = cand_row.shape[1]
    owners, holders = lax.axis_size("corpus"), lax.axis_size("blk")
    room = 2 * count * listed // owners
    passages = index.shape[0]
    width = count * tokens
    smem = pltpu.SMEM
    vmem = pl.BlockSpec(memory_space=pltpu.VMEM)
    dma = pltpu.SemaphoreType.DMA
    chunks = 16
    grads, losses = pl.pallas_call(
        functools.partial(kernel, owners, holders, room, chunks, neg_row.shape[1]),
        out_shape=[
            jax.ShapeDtypeStruct((count, tokens, dim), F32),
            jax.ShapeDtypeStruct((1, count), F32),
        ],
        in_specs=[vmem] * 5 + [pl.BlockSpec(memory_space=pl.ANY)],
        out_specs=[vmem, vmem],
        scratch_shapes=[
            pltpu.VMEM(index.shape, BF16),
            pltpu.VMEM((passages, dim, index.shape[1]), BF16),
            pltpu.VMEM((passages, 128), F32),
            pltpu.VMEM((owners, count, tokens, dim), BF16),
            pltpu.VMEM((count, tokens, dim), BF16),
            pltpu.VMEM((dim, width), BF16),
            pltpu.VMEM((room + 1, tokens, dim), BF16),
            pltpu.VMEM((room + 1, tokens, dim), BF16),
            pltpu.VMEM((room + 8, 128), F32),
            pltpu.VMEM((room + 8, 128), F32),
            pltpu.VMEM((dim, width), F32),
            pltpu.VMEM((8, width), F32),
            pltpu.VMEM((count, tokens, dim), F32),
            pltpu.VMEM((count, tokens, dim), F32),
            pltpu.VMEM((3, count, 128), F32),
            pltpu.VMEM((128, 128), F32),
            pltpu.VMEM((128, 128), F32),
            pltpu.VMEM((count * listed // 128, 128, 128), F32),
            pltpu.VMEM((count * listed // 128, 128, 128), F32),
            pltpu.VMEM((count * listed // 128, 128, 128), F32),
            pltpu.VMEM((owners, 8, 128), I32),
            pltpu.VMEM((owners, 8, 128), F32),
            pltpu.VMEM((owners, 8, 128), I32),
            pltpu.VMEM((owners, 8, 128), F32),
            pltpu.VMEM((holders, 8, 128), I32),
            pltpu.VMEM((8, 128), I32),
            pltpu.VMEM((owners, count, 2 * tokens, dim), BF16),
            pltpu.VMEM((owners, 2, count, 128), F32),
            pltpu.VMEM((owners, count, 2 * tokens, dim), BF16),
            pltpu.VMEM((owners, 2, count, 128), F32),
            smem((owners, 8, 128), I32),
            smem((owners, 8, 128), F32),
            smem((holders, 8, 128), I32),
            dma((chunks,)),
            *[dma((owners,)) for _ in range(6)],
            *[dma((holders,)) for _ in range(2)],
            *[dma((owners,)) for _ in range(4)],
            dma((3,)),
        ],
        compiler_params=pltpu.CompilerParams(
            collective_id=0, has_side_effects=True, vmem_limit_bytes=60 << 20
        ),
        name="distill",
    )(
        cand_owner.reshape(count, listed), cand_row, neg_row, teacher,
        queries.reshape(width, dim), index,
    )
    return losses.reshape(count), grads


def solution(mesh):
    both = ("corpus", "blk")
    return jax.shard_map(
        step,
        mesh=mesh,
        in_specs=(
            P(both, None, None), P("corpus", None, None), P(both, None, None),
            P(both, None), P(both, None), P(both, None),
        ),
        out_specs=(P(both), P(both, None, None)),
        check_vma=False,
    )
```

```python
import functools
import math

import jax
import jax.numpy as jnp
from jax import lax
from jax.experimental import pallas as pl
from jax.experimental.pallas import tpu as pltpu
from jax.sharding import PartitionSpec as P

MESH = pl.DeviceIdType.MESH
F32, BF16, I32 = jnp.float32, jnp.bfloat16, jnp.int32
EPS = 1e-6
SCALE = 10.0 * math.log2(math.e)
LN2 = math.log(2.0)
ROWS_NT = (((1,), (1,)), ((), ()))


def lane_sum_of_groups(x, group, lane, width):
    shift = group // 2
    while shift:
        x = x + jnp.where(
            (lane & shift) != 0, pltpu.roll(x, shift, 1), pltpu.roll(x, width - shift, 1)
        )
        shift //= 2
    return x


def transpose_pass(first, count, unroll, w_ref, inv_ref, tt_ref):
    def body(b, _):
        rows = [first + b * unroll + u for u in range(unroll)]
        wide = [jnp.transpose(w_ref[r]).astype(F32) for r in rows]
        inv = [lax.rsqrt(jnp.sum(x * x, axis=0, keepdims=True) + EPS) for x in wide]
        for u, r in enumerate(rows):
            inv_ref[pl.ds(r, 1)] = inv[u]
            tt_ref[r] = (wide[u] * (inv[u] * SCALE)).astype(BF16)
        return 0

    lax.fori_loop(0, count // unroll, body, 0)


def build_tables(owners, room, codes_end, names_ref, row_ref, target, turned, place, codes, wants, ends, tab_i, tab_f):
    count, listed = row_ref.shape
    lane = lax.broadcasted_iota(I32, (128, 128), 1)
    line = lax.broadcasted_iota(I32, (128, 128), 0)
    lane_f = lane.astype(F32)
    lower = (lane < line).astype(F32).astype(BF16)

    def flip(x):
        turned[...] = jnp.zeros_like(turned)
        turned[0:count, 0:listed] = x
        return jnp.transpose(turned[...])

    number = lax.broadcasted_iota(I32, row_ref.shape, 0)
    names = flip(names_ref[...].astype(F32))
    code = flip((row_ref[...] * count + number).astype(F32))
    want = flip(target)
    per = 128 // listed
    blocks = count // per
    offset = jnp.zeros((1, 128), F32)
    ends[...] = jnp.zeros_like(ends)
    for r in range(blocks):
        def column(x):
            return jnp.concatenate(
                [x[0:listed, r * per + i : r * per + i + 1] for i in range(per)], axis=0
            )

        hit = (column(names) == lane_f)
        ones = hit.astype(F32)
        rank = jnp.dot(lower, ones.astype(BF16), preferred_element_type=F32) + offset
        where = jnp.sum(jnp.where(hit, rank + lane_f * room, 0.0), axis=1, keepdims=True)
        place[r] = jnp.broadcast_to(where, (128, 128))
        codes[r] = jnp.broadcast_to(column(code), (128, 128))
        wants[r] = jnp.broadcast_to(column(want), (128, 128))
        for i in range(per):
            at = (i + 1) * listed - 1
            upto = rank[at : at + 1] + ones[at : at + 1]
            start = offset if i == 0 else before
            ends[r * per + i : r * per + i + 1] = jnp.where(
                upto > start, jnp.minimum(upto - 1.0, float(room)), float(room)
            )
            before = upto
        offset = before
    turned[...] = jnp.transpose(ends[...])
    tab_i[...] = jnp.zeros_like(tab_i)
    tab_f[...] = jnp.zeros_like(tab_f)
    mark = lax.broadcasted_iota(I32, (1, 128), 1)

    def one_owner(o, _):
        slot = lane_f + (o * room).astype(F32)
        sum_c = jnp.zeros((128, 128), F32)
        sum_w = jnp.zeros((128, 128), F32)
        for r in range(blocks):
            here = place[r] == slot
            sum_c = sum_c + jnp.where(here, codes[r], 0.0)
            sum_w = sum_w + jnp.where(here, wants[r], 0.0)
        c = jnp.clip(jnp.sum(sum_c, axis=0, keepdims=True).astype(I32), 0, codes_end - 1)
        whose = c & (count - 1)
        same = (whose == pltpu.roll(whose, 1, 1)) & (mark > 0)
        tab_i[o, 0:1] = c
        tab_i[o, 1:2] = jnp.clip(turned[pl.ds(o, 1)].astype(I32), 0, room)
        tab_f[o, 0:1] = jnp.sum(sum_w, axis=0, keepdims=True)
        tab_f[o, 1:2] = jnp.where(same, 1.0, 0.0)
        return 0

    lax.fori_loop(0, owners, one_owner, 0)


def negatives(first_step, last_step, unroll, rows_ref, each, tt_ref, qt_ref, acc_ref, sum_ref):
    width = qt_ref.shape[1]
    lane = lax.broadcasted_iota(I32, (1, width), 1)
    steps = each // unroll

    def body(b, _):
        holder, first = b // steps, lax.rem(b, steps) * unroll
        flipped = [tt_ref[rows_ref[holder, 0, first + u]] for u in range(unroll)]
        tiles = jnp.concatenate([jnp.transpose(t) for t in flipped], axis=0)
        sims = jnp.dot(tiles, qt_ref[...], preferred_element_type=F32)
        expo = jnp.exp2(sims)
        parts = [expo[u * 128 : (u + 1) * 128] for u in range(unroll)]
        logs = jnp.log2(
            jnp.concatenate([jnp.sum(x, axis=0, keepdims=True) for x in parts], axis=0)
        )
        top = jnp.exp2(lane_sum_of_groups(logs, 32, lane, width) * 0.1)
        factor = top * jnp.exp2(-logs)
        weights = jnp.concatenate(
            [(parts[u] * factor[u : u + 1]).astype(BF16) for u in range(unroll)], axis=0
        )
        acc_ref[...] += jnp.dot(
            jnp.concatenate(flipped, axis=1), weights, preferred_element_type=F32
        )
        sum_ref[0:1] += jnp.sum(top, axis=0, keepdims=True)
        return 0

    lax.fori_loop(first_step, last_step, body, 0)


def paired_dots(left, right):
    zero = jnp.zeros(left[0].shape, left[0].dtype)
    m = left[0].shape[0]
    out = []
    for i in range(0, len(left), 2):
        both = jnp.concatenate(
            [
                jnp.concatenate([left[i], zero], axis=1),
                jnp.concatenate([zero, left[i + 1]], axis=1),
            ],
            axis=0,
        )
        stacked = jnp.concatenate([right[i], right[i + 1]], axis=0)
        two = jnp.dot(both, stacked, preferred_element_type=F32)
        out += [two[:m], two[m:]]
    return out


def listed_pairs(src, room, unroll, group, tab_i, tab_f, w_ref, inv_ref, tt_ref, q_ref, pa, pb, p1, p2):
    zero = jnp.zeros((32, 128), F32)
    one = jnp.zeros((1, 1), F32)

    def body(b, carry):
        acc_a, acc_b, acc_1, acc_2 = carry
        ks = [b * unroll + u for u in range(unroll)]
        cs = [tab_i[src, 0, k] for k in ks]
        sims, expo, totals, weights, back, score, top, flat = [{} for _ in range(8)]
        steps = unroll // group
        for t in range(steps + 3):
            us = range(t * group, (t + 1) * group)
            if t < steps:
                dots = paired_dots([q_ref[cs[u] & 15] for u in us], [tt_ref[cs[u] >> 4] for u in us])
                sims.update(zip(us, dots))
            us = range((t - 1) * group, t * group)
            if 0 <= t - 1 < steps:
                for u in us:
                    expo[u] = jnp.exp2(sims.pop(u))
                    totals[u] = jnp.sum(expo[u], axis=-1, keepdims=True)
                for u in us:
                    weights[u] = (expo.pop(u) * inv_ref[pl.ds(cs[u] >> 4, 1)]).astype(BF16)
            us = range((t - 2) * group, (t - 1) * group)
            if 0 <= t - 2 < steps:
                dots = paired_dots([weights.pop(u) for u in us], [w_ref[cs[u] >> 4] for u in us])
                back.update(zip(us, dots))
                logs = {u: jnp.log2(totals.pop(u)) for u in us}
                for u in us:
                    flat[u] = jnp.exp2(-logs[u])
                for u in us:
                    score[u] = jnp.sum(logs[u], axis=0, keepdims=True) * 0.1
                for u in us:
                    top[u] = jnp.exp2(score[u])
            us = range((t - 3) * group, (t - 2) * group)
            if 0 <= t - 3 < steps:
                for u in us:
                    k = ks[u]
                    here = back.pop(u) * flat.pop(u)
                    target, stay = tab_f[src, 0, k], tab_f[src, 1, k]
                    acc_a = acc_a * stay + here * top[u]
                    acc_b = acc_b * stay + here * target
                    acc_1 = acc_1 * stay + top[u]
                    acc_2 = acc_2 * stay + score[u] * target
                    pa[k] = acc_a.astype(BF16)
                    pb[k] = acc_b.astype(BF16)
                    p1[pl.ds(k, 1)] = jnp.broadcast_to(acc_1, (1, 128))
                    p2[pl.ds(k, 1)] = jnp.broadcast_to(acc_2, (1, 128))
        return acc_a, acc_b, acc_1, acc_2

    lax.fori_loop(0, room // unroll, body, (zero, zero, one, one))


def kernel(
    owners, holders, room, chunks, sampled,
    names_ref, row_ref, neg_ref, teacher_ref, q_ref, index_ref,
    grad_ref, loss_ref,
    w, tt, inv, qall, qcur, qt, pa, pb, p1, p2, acc, nsum, flat_a, flat_s, stats,
    turned, ends, place, codes, wants, tab_i, tab_f, all_i, all_f, all_n, neg_own,
    back_buf, sum_buf, got, got_sum,
    code_s, mark_s, rows_s,
    load_sem, q_send, q_recv, i_send, i_recv, f_send, f_recv, n_send, n_recv,
    b_send, b_recv, s_send, s_recv, smem_sem,
):
    me = lax.axis_index("corpus")
    seat = lax.axis_index("blk")
    count, tokens = qcur.shape[0], qcur.shape[1]
    part = w.shape[0] // chunks
    barrier = pltpu.get_barrier_semaphore()

    def each(first, last, act):
        def body(k, _):
            act(k)
            return 0

        lax.fori_loop(first, last, body, 0)

    def loads(j):
        rows = pl.ds(j * part, part)
        return pltpu.make_async_copy(index_ref.at[rows], w.at[rows], load_sem.at[j])

    side = math.isqrt(owners)
    own = owners // 2

    def shifted(m, sign):
        dy = side // 2 + m // side
        dz = dy + lax.rem(m, side)
        y = lax.rem(me // side + sign * lax.rem(dy, side) + side, side)
        z = lax.rem(lax.rem(me, side) + sign * lax.rem(dz, side) + side, side)
        return y * side + z

    def owner(m):
        return {"corpus": shifted(m, 1)}

    def peers(act):
        each(0, own, act)
        each(own + 1, owners, act)

    def holder(k):
        return {"blk": lax.rem(seat + k, holders)}

    def remote(src, dst, send, recv, k, device):
        return pltpu.make_async_remote_copy(
            src_ref=src, dst_ref=dst, send_sem=send.at[k], recv_sem=recv.at[k],
            device_id=device, device_id_type=MESH,
        )

    def greet(device):
        pl.semaphore_signal(barrier, inc=1, device_id=device, device_id_type=MESH)

    each(0, chunks, lambda j: loads(j).start())
    peers(lambda k: greet(owner(k)))
    each(1, holders, lambda k: greet(holder(k)))

    wide = q_ref[...].astype(F32)
    radius = jnp.sqrt(jnp.sum(wide * wide, axis=-1, keepdims=True) + EPS)
    rounded = (wide / radius).astype(BF16)
    qall[me] = rounded.reshape(qcur.shape)
    qt[...] = jnp.transpose(rounded)
    neg_own[...] = jnp.zeros_like(neg_own)
    neg_own[0:1, 0:sampled] = neg_ref[...]
    all_n[seat] = neg_own[...]

    pl.semaphore_wait(barrier, owners + holders - 2)

    def n_copy(k):
        return remote(neg_own, all_n.at[seat], n_send, n_recv, k, holder(k))

    def q_copy(k):
        return remote(qall.at[me], qall.at[me], q_send, q_recv, k, owner(k))

    def table_copies(k):
        to = shifted(k, 1)
        return (
            remote(tab_i.at[to], all_i.at[me], i_send, i_recv, k, owner(k)),
            remote(tab_f.at[to], all_f.at[me], f_send, f_recv, k, owner(k)),
        )

    each(1, holders, lambda k: n_copy(k).start())
    peers(lambda k: q_copy(k).start())

    teacher = teacher_ref[...]
    log_target = teacher - jnp.log(jnp.sum(jnp.exp(teacher), axis=1, keepdims=True))
    target = jnp.exp(log_target)
    stats[0] = jnp.broadcast_to(jnp.sum(target * log_target, axis=1, keepdims=True), (count, 128))
    stats[1] = jnp.broadcast_to(jnp.sum(target, axis=1, keepdims=True), (count, 128))
    build_tables(
        owners, room, w.shape[0] * count, names_ref, row_ref, target, turned, place, codes, wants, ends, tab_i, tab_f
    )
    all_i[me] = tab_i[me]
    all_f[me] = tab_f[me]
    peers(lambda k: [copy.start() for copy in table_copies(k)])

    def prepare(j):
        loads(j).wait()
        transpose_pass(j * part, part, 8, w, inv, tt)

    each(0, chunks, prepare)
    each(1, holders, lambda k: n_copy(k).wait())
    peers(lambda k: [copy.wait() for copy in table_copies(k)])
    moves = [
        pltpu.make_async_copy(all_n, rows_s, smem_sem.at[0]),
        pltpu.make_async_copy(all_i, code_s, smem_sem.at[1]),
        pltpu.make_async_copy(all_f, mark_s, smem_sem.at[2]),
    ]
    for move in moves:
        move.start()
    for move in moves:
        move.wait()
    acc[...] = jnp.zeros_like(acc)
    nsum[...] = jnp.zeros_like(nsum)
    neg_steps = holders * sampled // 8
    early = 0
    negatives(0, early, 8, rows_s, sampled, tt, qt, acc, nsum)

    pa[room] = jnp.zeros((tokens, 128), BF16)
    pb[room] = jnp.zeros((tokens, 128), BF16)
    p1[room : room + 8] = jnp.zeros((8, 128), F32)
    p2[room : room + 8] = jnp.zeros((8, 128), F32)

    def back_copies(k):
        to = {"corpus": shifted(k, -1)}
        return (
            remote(back_buf.at[k], got.at[k], b_send, b_recv, k, to),
            remote(sum_buf.at[k], got_sum.at[k], s_send, s_recv, k, to),
        )

    def source(k):
        src = shifted(k, -1)

        @pl.when(k != own)
        def _():
            q_copy(k).wait_recv()

        qcur[...] = qall[src]
        listed_pairs(src, room, 64, 8, code_s, mark_s, w, inv, tt, qcur, pa, pb, p1, p2)

        def extract(q, _):
            at = code_s[src, 1, q]
            back_buf[k, q, 0:tokens] = pa[at]
            back_buf[k, q, tokens : 2 * tokens] = pb[at]
            sum_buf[k, 0, pl.ds(q, 1)] = p1[pl.ds(at, 1)]
            sum_buf[k, 1, pl.ds(q, 1)] = p2[pl.ds(at, 1)]
            return 0

        lax.fori_loop(0, count, extract, 0, unroll=4)

        @pl.when(k != own)
        def _():
            for copy in back_copies(k):
                copy.start()

    each(0, owners, source)
    negatives(early, neg_steps, 8, rows_s, sampled, tt, qt, acc, nsum)

    turned_a = jnp.transpose(acc[...]) * (1.0 / SCALE)
    turned_s = jnp.transpose(jnp.broadcast_to(nsum[0:1], (128, count * tokens)))
    flat_a[...] = turned_a.reshape(flat_a.shape)
    flat_s[...] = turned_s.reshape(flat_s.shape)

    peers(lambda k: [copy.wait() for copy in back_copies(k)])
    peers(lambda k: q_copy(k).wait_send())
    sums = sum_buf[own]
    others = [k for k in range(owners) if k != own]
    for k in others:
        sums = sums + got_sum[k]
    p1[0:count] = sums[0]
    p2[0:count] = sums[1]

    def finish(q, _):
        part_a = flat_a[q] + back_buf[own, q, 0:tokens].astype(F32)
        part_b = back_buf[own, q, tokens : 2 * tokens].astype(F32)
        for k in others:
            part_a = part_a + got[k, q, 0:tokens].astype(F32)
            part_b = part_b + got[k, q, tokens : 2 * tokens].astype(F32)
        whole = flat_s[q] + p1[pl.ds(q, 1)]
        pulled = part_a / whole - part_b
        raw = q_ref[pl.ds(pl.multiple_of(q * tokens, tokens), tokens)].astype(F32)
        rad = jnp.sqrt(jnp.sum(raw * raw, axis=-1, keepdims=True) + EPS)
        unit = raw / rad
        along = jnp.sum(unit * pulled, axis=-1, keepdims=True)
        grad_ref[q] = (pulled - unit * along) / rad
        one = pl.ds(q, 1)
        stats[2, one] = stats[0, one] - LN2 * p2[one] + jnp.log(whole[0:1]) * stats[1, one]
        return 0

    lax.fori_loop(0, count, finish, 0, unroll=2)
    turned[...] = jnp.zeros_like(turned)
    turned[0:count] = stats[2]
    loss_ref[...] = jnp.transpose(turned[...])[0:1, 0:count]


def step(queries, index, cand_owner, cand_row, neg_row, teacher):
    count, tokens, dim = queries.shape
    listed = cand_row.shape[1]
    owners, holders = lax.axis_size("corpus"), lax.axis_size("blk")
    room = 2 * count * listed // owners
    passages = index.shape[0]
    width = count * tokens
    smem = pltpu.SMEM
    vmem = pl.BlockSpec(memory_space=pltpu.VMEM)
    dma = pltpu.SemaphoreType.DMA
    chunks = 16
    grads, losses = pl.pallas_call(
        functools.partial(kernel, owners, holders, room, chunks, neg_row.shape[1]),
        out_shape=[
            jax.ShapeDtypeStruct((count, tokens, dim), F32),
            jax.ShapeDtypeStruct((1, count), F32),
        ],
        in_specs=[vmem] * 5 + [pl.BlockSpec(memory_space=pl.ANY)],
        out_specs=[vmem, vmem],
        scratch_shapes=[
            pltpu.VMEM(index.shape, BF16),
            pltpu.VMEM((passages, dim, index.shape[1]), BF16),
            pltpu.VMEM((passages, 128), F32),
            pltpu.VMEM((owners, count, tokens, dim), BF16),
            pltpu.VMEM((count, tokens, dim), BF16),
            pltpu.VMEM((dim, width), BF16),
            pltpu.VMEM((room + 1, tokens, dim), BF16),
            pltpu.VMEM((room + 1, tokens, dim), BF16),
            pltpu.VMEM((room + 8, 128), F32),
            pltpu.VMEM((room + 8, 128), F32),
            pltpu.VMEM((dim, width), F32),
            pltpu.VMEM((8, width), F32),
            pltpu.VMEM((count, tokens, dim), F32),
            pltpu.VMEM((count, tokens, dim), F32),
            pltpu.VMEM((3, count, 128), F32),
            pltpu.VMEM((128, 128), F32),
            pltpu.VMEM((128, 128), F32),
            pltpu.VMEM((count * listed // 128, 128, 128), F32),
            pltpu.VMEM((count * listed // 128, 128, 128), F32),
            pltpu.VMEM((count * listed // 128, 128, 128), F32),
            pltpu.VMEM((owners, 8, 128), I32),
            pltpu.VMEM((owners, 8, 128), F32),
            pltpu.VMEM((owners, 8, 128), I32),
            pltpu.VMEM((owners, 8, 128), F32),
            pltpu.VMEM((holders, 8, 128), I32),
            pltpu.VMEM((8, 128), I32),
            pltpu.VMEM((owners, count, 2 * tokens, dim), BF16),
            pltpu.VMEM((owners, 2, count, 128), F32),
            pltpu.VMEM((owners, count, 2 * tokens, dim), BF16),
            pltpu.VMEM((owners, 2, count, 128), F32),
            smem((owners, 8, 128), I32),
            smem((owners, 8, 128), F32),
            smem((holders, 8, 128), I32),
            dma((chunks,)),
            *[dma((owners,)) for _ in range(6)],
            *[dma((holders,)) for _ in range(2)],
            *[dma((owners,)) for _ in range(4)],
            dma((3,)),
        ],
        compiler_params=pltpu.CompilerParams(
            collective_id=0, has_side_effects=True, vmem_limit_bytes=60 << 20
        ),
        name="distill",
    )(
        cand_owner.reshape(count, listed), cand_row, neg_row, teacher,
        queries.reshape(width, dim), index,
    )
    return losses.reshape(count), grads


def solution(mesh):
    both = ("corpus", "blk")
    return jax.shard_map(
        step,
        mesh=mesh,
        in_specs=(
            P(both, None, None), P("corpus", None, None), P(both, None, None),
            P(both, None), P(both, None), P(both, None),
        ),
        out_specs=(P(both), P(both, None, None)),
        check_vma=False,
    )
```

```python
import functools
import math

import jax
import jax.numpy as jnp
from jax import lax
from jax.experimental import pallas as pl
from jax.experimental.pallas import tpu as pltpu
from jax.sharding import PartitionSpec as P

MESH = pl.DeviceIdType.MESH
F32, BF16, I32 = jnp.float32, jnp.bfloat16, jnp.int32
EPS = 1e-6
SCALE = 10.0 * math.log2(math.e)
LN2 = math.log(2.0)
ROWS_NT = (((1,), (1,)), ((), ()))


def lane_sum_of_groups(x, group, lane, width):
    shift = group // 2
    while shift:
        x = x + jnp.where(
            (lane & shift) != 0, pltpu.roll(x, shift, 1), pltpu.roll(x, width - shift, 1)
        )
        shift //= 2
    return x


def transpose_pass(first, count, unroll, w_ref, inv_ref, tt_ref):
    def body(b, _):
        rows = [first + b * unroll + u for u in range(unroll)]
        wide = [jnp.transpose(w_ref[r]).astype(F32) for r in rows]
        inv = [lax.rsqrt(jnp.sum(x * x, axis=0, keepdims=True) + EPS) for x in wide]
        for u, r in enumerate(rows):
            inv_ref[pl.ds(r, 1)] = inv[u]
            tt_ref[r] = (wide[u] * (inv[u] * SCALE)).astype(BF16)
        return 0

    lax.fori_loop(0, count // unroll, body, 0)


def build_tables(owners, room, codes_end, names_ref, row_ref, target, turned, place, codes, wants, ends, tab_i, tab_f):
    count, listed = row_ref.shape
    lane = lax.broadcasted_iota(I32, (128, 128), 1)
    line = lax.broadcasted_iota(I32, (128, 128), 0)
    lane_f = lane.astype(F32)
    lower = (lane < line).astype(F32).astype(BF16)

    def flip(x):
        turned[...] = jnp.zeros_like(turned)
        turned[0:count, 0:listed] = x
        return jnp.transpose(turned[...])

    number = lax.broadcasted_iota(I32, row_ref.shape, 0)
    names = flip(names_ref[...].astype(F32))
    code = flip((row_ref[...] * count + number).astype(F32))
    want = flip(target)
    per = 128 // listed
    blocks = count // per
    offset = jnp.zeros((1, 128), F32)
    ends[...] = jnp.zeros_like(ends)
    for r in range(blocks):
        def column(x):
            return jnp.concatenate(
                [x[0:listed, r * per + i : r * per + i + 1] for i in range(per)], axis=0
            )

        hit = (column(names) == lane_f)
        ones = hit.astype(F32)
        rank = jnp.dot(lower, ones.astype(BF16), preferred_element_type=F32) + offset
        where = jnp.sum(jnp.where(hit, rank + lane_f * room, 0.0), axis=1, keepdims=True)
        place[r] = jnp.broadcast_to(where, (128, 128))
        codes[r] = jnp.broadcast_to(column(code), (128, 128))
        wants[r] = jnp.broadcast_to(column(want), (128, 128))
        for i in range(per):
            at = (i + 1) * listed - 1
            upto = rank[at : at + 1] + ones[at : at + 1]
            start = offset if i == 0 else before
            ends[r * per + i : r * per + i + 1] = jnp.where(
                upto > start, jnp.minimum(upto - 1.0, float(room)), float(room)
            )
            before = upto
        offset = before
    turned[...] = jnp.transpose(ends[...])
    tab_i[...] = jnp.zeros_like(tab_i)
    tab_f[...] = jnp.zeros_like(tab_f)
    mark = lax.broadcasted_iota(I32, (1, 128), 1)

    def one_owner(o, _):
        slot = lane_f + (o * room).astype(F32)
        sum_c = jnp.zeros((128, 128), F32)
        sum_w = jnp.zeros((128, 128), F32)
        for r in range(blocks):
            here = place[r] == slot
            sum_c = sum_c + jnp.where(here, codes[r], 0.0)
            sum_w = sum_w + jnp.where(here, wants[r], 0.0)
        c = jnp.clip(jnp.sum(sum_c, axis=0, keepdims=True).astype(I32), 0, codes_end - 1)
        whose = c & (count - 1)
        same = (whose == pltpu.roll(whose, 1, 1)) & (mark > 0)
        tab_i[o, 0:1] = c
        tab_i[o, 1:2] = jnp.clip(turned[pl.ds(o, 1)].astype(I32), 0, room)
        tab_f[o, 0:1] = jnp.sum(sum_w, axis=0, keepdims=True)
        tab_f[o, 1:2] = jnp.where(same, 1.0, 0.0)
        return 0

    lax.fori_loop(0, owners, one_owner, 0)


def negatives(first_step, last_step, unroll, rows_ref, each, tt_ref, qt_ref, acc_ref, sum_ref):
    width = qt_ref.shape[1]
    lane = lax.broadcasted_iota(I32, (1, width), 1)
    steps = each // unroll

    def body(b, _):
        holder, first = b // steps, lax.rem(b, steps) * unroll
        flipped = [tt_ref[rows_ref[holder, 0, first + u]] for u in range(unroll)]
        tiles = jnp.concatenate([jnp.transpose(t) for t in flipped], axis=0)
        sims = jnp.dot(tiles, qt_ref[...], preferred_element_type=F32)
        expo = jnp.exp2(sims)
        parts = [expo[u * 128 : (u + 1) * 128] for u in range(unroll)]
        logs = jnp.log2(
            jnp.concatenate([jnp.sum(x, axis=0, keepdims=True) for x in parts], axis=0)
        )
        top = jnp.exp2(lane_sum_of_groups(logs, 32, lane, width) * 0.1)
        factor = top * jnp.exp2(-logs)
        weights = jnp.concatenate(
            [(parts[u] * factor[u : u + 1]).astype(BF16) for u in range(unroll)], axis=0
        )
        acc_ref[...] += jnp.dot(
            jnp.concatenate(flipped, axis=1), weights, preferred_element_type=F32
        )
        sum_ref[0:1] += jnp.sum(top, axis=0, keepdims=True)
        return 0

    lax.fori_loop(first_step, last_step, body, 0)


def paired_dots(left, right):
    zero = jnp.zeros(left[0].shape, left[0].dtype)
    m = left[0].shape[0]
    out = []
    for i in range(0, len(left), 2):
        both = jnp.concatenate(
            [
                jnp.concatenate([left[i], zero], axis=1),
                jnp.concatenate([zero, left[i + 1]], axis=1),
            ],
            axis=0,
        )
        stacked = jnp.concatenate([right[i], right[i + 1]], axis=0)
        two = jnp.dot(both, stacked, preferred_element_type=F32)
        out += [two[:m], two[m:]]
    return out


def listed_pairs(src, room, unroll, group, tab_i, tab_f, w_ref, inv_ref, tt_ref, q_ref, pa, pb, p1, p2):
    zero = jnp.zeros((32, 128), F32)
    one = jnp.zeros((1, 1), F32)

    def body(b, carry):
        acc_a, acc_b, acc_1, acc_2 = carry
        ks = [b * unroll + u for u in range(unroll)]
        cs = [tab_i[src, 0, k] for k in ks]
        sims, expo, totals, weights, back, score, top, flat = [{} for _ in range(8)]
        steps = unroll // group
        for t in range(steps + 3):
            us = range(t * group, (t + 1) * group)
            if t < steps:
                dots = paired_dots([q_ref[cs[u] & 15] for u in us], [tt_ref[cs[u] >> 4] for u in us])
                sims.update(zip(us, dots))
            us = range((t - 1) * group, t * group)
            if 0 <= t - 1 < steps:
                for u in us:
                    expo[u] = jnp.exp2(sims.pop(u))
                    totals[u] = jnp.sum(expo[u], axis=-1, keepdims=True)
                for u in us:
                    weights[u] = (expo.pop(u) * inv_ref[pl.ds(cs[u] >> 4, 1)]).astype(BF16)
            us = range((t - 2) * group, (t - 1) * group)
            if 0 <= t - 2 < steps:
                dots = paired_dots([weights.pop(u) for u in us], [w_ref[cs[u] >> 4] for u in us])
                back.update(zip(us, dots))
                logs = {u: jnp.log2(totals.pop(u)) for u in us}
                for u in us:
                    flat[u] = jnp.exp2(-logs[u])
                for u in us:
                    score[u] = jnp.sum(logs[u], axis=0, keepdims=True) * 0.1
                for u in us:
                    top[u] = jnp.exp2(score[u])
            us = range((t - 3) * group, (t - 2) * group)
            if 0 <= t - 3 < steps:
                for u in us:
                    k = ks[u]
                    here = back.pop(u) * flat.pop(u)
                    target, stay = tab_f[src, 0, k], tab_f[src, 1, k]
                    acc_a = acc_a * stay + here * top[u]
                    acc_b = acc_b * stay + here * target
                    acc_1 = acc_1 * stay + top[u]
                    acc_2 = acc_2 * stay + score[u] * target
                    pa[k] = acc_a.astype(BF16)
                    pb[k] = acc_b.astype(BF16)
                    p1[pl.ds(k, 1)] = jnp.broadcast_to(acc_1, (1, 128))
                    p2[pl.ds(k, 1)] = jnp.broadcast_to(acc_2, (1, 128))
        return acc_a, acc_b, acc_1, acc_2

    lax.fori_loop(0, room // unroll, body, (zero, zero, one, one))


def kernel(
    owners, holders, room, chunks, sampled,
    names_ref, row_ref, neg_ref, teacher_ref, q_ref, index_ref,
    grad_ref, loss_ref,
    w, tt, inv, qall, qcur, qt, pa, pb, p1, p2, acc, nsum, flat_a, flat_s, stats,
    turned, ends, place, codes, wants, tab_i, tab_f, all_i, all_f, all_n, neg_own,
    back_buf, sum_buf, got, got_sum,
    code_s, mark_s, rows_s,
    load_sem, q_send, q_recv, i_send, i_recv, f_send, f_recv, n_send, n_recv,
    b_send, b_recv, s_send, s_recv, smem_sem,
):
    me = lax.axis_index("corpus")
    seat = lax.axis_index("blk")
    count, tokens = qcur.shape[0], qcur.shape[1]
    part = w.shape[0] // chunks
    barrier = pltpu.get_barrier_semaphore()

    def each(first, last, act):
        def body(k, _):
            act(k)
            return 0

        lax.fori_loop(first, last, body, 0)

    def loads(j):
        rows = pl.ds(j * part, part)
        return pltpu.make_async_copy(index_ref.at[rows], w.at[rows], load_sem.at[j])

    side = math.isqrt(owners)
    own = side // 2

    def shifted(m, sign):
        dy = side // 2 + lax.rem(m, side)
        dz = dy + m // side
        y = lax.rem(me // side + sign * lax.rem(dy, side) + side, side)
        z = lax.rem(lax.rem(me, side) + sign * lax.rem(dz, side) + side, side)
        return y * side + z

    def owner(m):
        return {"corpus": shifted(m, 1)}

    def peers(act):
        each(0, own, act)
        each(own + 1, owners, act)

    def holder(k):
        return {"blk": lax.rem(seat + k, holders)}

    def remote(src, dst, send, recv, k, device):
        return pltpu.make_async_remote_copy(
            src_ref=src, dst_ref=dst, send_sem=send.at[k], recv_sem=recv.at[k],
            device_id=device, device_id_type=MESH,
        )

    def greet(device):
        pl.semaphore_signal(barrier, inc=1, device_id=device, device_id_type=MESH)

    each(0, chunks, lambda j: loads(j).start())
    peers(lambda k: greet(owner(k)))
    each(1, holders, lambda k: greet(holder(k)))

    wide = q_ref[...].astype(F32)
    radius = jnp.sqrt(jnp.sum(wide * wide, axis=-1, keepdims=True) + EPS)
    rounded = (wide / radius).astype(BF16)
    qall[me] = rounded.reshape(qcur.shape)
    qt[...] = jnp.transpose(rounded)
    neg_own[...] = jnp.zeros_like(neg_own)
    neg_own[0:1, 0:sampled] = neg_ref[...]
    all_n[seat] = neg_own[...]

    pl.semaphore_wait(barrier, owners + holders - 2)

    def n_copy(k):
        return remote(neg_own, all_n.at[seat], n_send, n_recv, k, holder(k))

    def q_copy(k):
        return remote(qall.at[me], qall.at[me], q_send, q_recv, k, owner(k))

    def table_copies(k):
        to = shifted(k, 1)
        return (
            remote(tab_i.at[to], all_i.at[me], i_send, i_recv, k, owner(k)),
            remote(tab_f.at[to], all_f.at[me], f_send, f_recv, k, owner(k)),
        )

    each(1, holders, lambda k: n_copy(k).start())
    at_once = 4
    each(0, own, lambda k: q_copy(k).start())
    each(own + 1, at_once, lambda k: q_copy(k).start())

    teacher = teacher_ref[...]
    log_target = teacher - jnp.log(jnp.sum(jnp.exp(teacher), axis=1, keepdims=True))
    target = jnp.exp(log_target)
    stats[0] = jnp.broadcast_to(jnp.sum(target * log_target, axis=1, keepdims=True), (count, 128))
    stats[1] = jnp.broadcast_to(jnp.sum(target, axis=1, keepdims=True), (count, 128))
    build_tables(
        owners, room, w.shape[0] * count, names_ref, row_ref, target, turned, place, codes, wants, ends, tab_i, tab_f
    )
    all_i[me] = tab_i[me]
    all_f[me] = tab_f[me]
    peers(lambda k: [copy.start() for copy in table_copies(k)])

    def prepare(j):
        @pl.when(j < owners - at_once)
        def _():
            q_copy(at_once + j).start()

        loads(j).wait()
        transpose_pass(j * part, part, 8, w, inv, tt)

    each(0, chunks, prepare)
    each(1, holders, lambda k: n_copy(k).wait())
    peers(lambda k: [copy.wait() for copy in table_copies(k)])
    moves = [
        pltpu.make_async_copy(all_n, rows_s, smem_sem.at[0]),
        pltpu.make_async_copy(all_i, code_s, smem_sem.at[1]),
        pltpu.make_async_copy(all_f, mark_s, smem_sem.at[2]),
    ]
    for move in moves:
        move.start()
    for move in moves:
        move.wait()
    acc[...] = jnp.zeros_like(acc)
    nsum[...] = jnp.zeros_like(nsum)
    neg_steps = holders * sampled // 8
    early = 0
    negatives(0, early, 8, rows_s, sampled, tt, qt, acc, nsum)

    pa[room] = jnp.zeros((tokens, 128), BF16)
    pb[room] = jnp.zeros((tokens, 128), BF16)
    p1[room : room + 8] = jnp.zeros((8, 128), F32)
    p2[room : room + 8] = jnp.zeros((8, 128), F32)

    def back_copies(k):
        to = {"corpus": shifted(k, -1)}
        return (
            remote(back_buf.at[k], got.at[k], b_send, b_recv, k, to),
            remote(sum_buf.at[k], got_sum.at[k], s_send, s_recv, k, to),
        )

    def source(k):
        src = shifted(k, -1)

        @pl.when(k != own)
        def _():
            q_copy(k).wait_recv()

        qcur[...] = qall[src]
        listed_pairs(src, room, 64, 8, code_s, mark_s, w, inv, tt, qcur, pa, pb, p1, p2)

        def extract(q, _):
            at = code_s[src, 1, q]
            back_buf[k, q, 0:tokens] = pa[at]
            back_buf[k, q, tokens : 2 * tokens] = pb[at]
            sum_buf[k, 0, pl.ds(q, 1)] = p1[pl.ds(at, 1)]
            sum_buf[k, 1, pl.ds(q, 1)] = p2[pl.ds(at, 1)]
            return 0

        lax.fori_loop(0, count, extract, 0, unroll=4)

        @pl.when(k != own)
        def _():
            for copy in back_copies(k):
                copy.start()

    each(0, owners, source)
    negatives(early, neg_steps, 8, rows_s, sampled, tt, qt, acc, nsum)

    turned_a = jnp.transpose(acc[...]) * (1.0 / SCALE)
    turned_s = jnp.transpose(jnp.broadcast_to(nsum[0:1], (128, count * tokens)))
    flat_a[...] = turned_a.reshape(flat_a.shape)
    flat_s[...] = turned_s.reshape(flat_s.shape)

    peers(lambda k: [copy.wait() for copy in back_copies(k)])
    peers(lambda k: q_copy(k).wait_send())
    sums = sum_buf[own]
    others = [k for k in range(owners) if k != own]
    for k in others:
        sums = sums + got_sum[k]
    p1[0:count] = sums[0]
    p2[0:count] = sums[1]

    def finish(q, _):
        part_a = flat_a[q] + back_buf[own, q, 0:tokens].astype(F32)
        part_b = back_buf[own, q, tokens : 2 * tokens].astype(F32)
        for k in others:
            part_a = part_a + got[k, q, 0:tokens].astype(F32)
            part_b = part_b + got[k, q, tokens : 2 * tokens].astype(F32)
        whole = flat_s[q] + p1[pl.ds(q, 1)]
        pulled = part_a / whole - part_b
        raw = q_ref[pl.ds(pl.multiple_of(q * tokens, tokens), tokens)].astype(F32)
        rad = jnp.sqrt(jnp.sum(raw * raw, axis=-1, keepdims=True) + EPS)
        unit = raw / rad
        along = jnp.sum(unit * pulled, axis=-1, keepdims=True)
        grad_ref[q] = (pulled - unit * along) / rad
        one = pl.ds(q, 1)
        stats[2, one] = stats[0, one] - LN2 * p2[one] + jnp.log(whole[0:1]) * stats[1, one]
        return 0

    lax.fori_loop(0, count, finish, 0, unroll=2)
    turned[...] = jnp.zeros_like(turned)
    turned[0:count] = stats[2]
    loss_ref[...] = jnp.transpose(turned[...])[0:1, 0:count]


def step(queries, index, cand_owner, cand_row, neg_row, teacher):
    count, tokens, dim = queries.shape
    listed = cand_row.shape[1]
    owners, holders = lax.axis_size("corpus"), lax.axis_size("blk")
    room = 2 * count * listed // owners
    passages = index.shape[0]
    width = count * tokens
    smem = pltpu.SMEM
    vmem = pl.BlockSpec(memory_space=pltpu.VMEM)
    dma = pltpu.SemaphoreType.DMA
    chunks = 16
    grads, losses = pl.pallas_call(
        functools.partial(kernel, owners, holders, room, chunks, neg_row.shape[1]),
        out_shape=[
            jax.ShapeDtypeStruct((count, tokens, dim), F32),
            jax.ShapeDtypeStruct((1, count), F32),
        ],
        in_specs=[vmem] * 5 + [pl.BlockSpec(memory_space=pl.ANY)],
        out_specs=[vmem, vmem],
        scratch_shapes=[
            pltpu.VMEM(index.shape, BF16),
            pltpu.VMEM((passages, dim, index.shape[1]), BF16),
            pltpu.VMEM((passages, 128), F32),
            pltpu.VMEM((owners, count, tokens, dim), BF16),
            pltpu.VMEM((count, tokens, dim), BF16),
            pltpu.VMEM((dim, width), BF16),
            pltpu.VMEM((room + 1, tokens, dim), BF16),
            pltpu.VMEM((room + 1, tokens, dim), BF16),
            pltpu.VMEM((room + 8, 128), F32),
            pltpu.VMEM((room + 8, 128), F32),
            pltpu.VMEM((dim, width), F32),
            pltpu.VMEM((8, width), F32),
            pltpu.VMEM((count, tokens, dim), F32),
            pltpu.VMEM((count, tokens, dim), F32),
            pltpu.VMEM((3, count, 128), F32),
            pltpu.VMEM((128, 128), F32),
            pltpu.VMEM((128, 128), F32),
            pltpu.VMEM((count * listed // 128, 128, 128), F32),
            pltpu.VMEM((count * listed // 128, 128, 128), F32),
            pltpu.VMEM((count * listed // 128, 128, 128), F32),
            pltpu.VMEM((owners, 8, 128), I32),
            pltpu.VMEM((owners, 8, 128), F32),
            pltpu.VMEM((owners, 8, 128), I32),
            pltpu.VMEM((owners, 8, 128), F32),
            pltpu.VMEM((holders, 8, 128), I32),
            pltpu.VMEM((8, 128), I32),
            pltpu.VMEM((owners, count, 2 * tokens, dim), BF16),
            pltpu.VMEM((owners, 2, count, 128), F32),
            pltpu.VMEM((owners, count, 2 * tokens, dim), BF16),
            pltpu.VMEM((owners, 2, count, 128), F32),
            smem((owners, 8, 128), I32),
            smem((owners, 8, 128), F32),
            smem((holders, 8, 128), I32),
            dma((chunks,)),
            *[dma((owners,)) for _ in range(6)],
            *[dma((holders,)) for _ in range(2)],
            *[dma((owners,)) for _ in range(4)],
            dma((3,)),
        ],
        compiler_params=pltpu.CompilerParams(
            collective_id=0, has_side_effects=True, vmem_limit_bytes=60 << 20
        ),
        name="distill",
    )(
        cand_owner.reshape(count, listed), cand_row, neg_row, teacher,
        queries.reshape(width, dim), index,
    )
    return losses.reshape(count), grads


def solution(mesh):
    both = ("corpus", "blk")
    return jax.shard_map(
        step,
        mesh=mesh,
        in_specs=(
            P(both, None, None), P("corpus", None, None), P(both, None, None),
            P(both, None), P(both, None), P(both, None),
        ),
        out_specs=(P(both), P(both, None, None)),
        check_vma=False,
    )
```

```python
import functools
import math

import jax
import jax.numpy as jnp
from jax import lax
from jax.experimental import pallas as pl
from jax.experimental.pallas import tpu as pltpu
from jax.sharding import PartitionSpec as P

MESH = pl.DeviceIdType.MESH
F32, BF16, I32 = jnp.float32, jnp.bfloat16, jnp.int32
EPS = 1e-6
SCALE = 10.0 * math.log2(math.e)
LN2 = math.log(2.0)
ROWS_NT = (((1,), (1,)), ((), ()))


def lane_sum_of_groups(x, group, lane, width):
    shift = group // 2
    while shift:
        x = x + jnp.where(
            (lane & shift) != 0, pltpu.roll(x, shift, 1), pltpu.roll(x, width - shift, 1)
        )
        shift //= 2
    return x


def transpose_pass(first, count, unroll, w_ref, inv_ref, tt_ref):
    def body(b, _):
        rows = [first + b * unroll + u for u in range(unroll)]
        wide = [jnp.transpose(w_ref[r]).astype(F32) for r in rows]
        inv = [lax.rsqrt(jnp.sum(x * x, axis=0, keepdims=True) + EPS) for x in wide]
        for u, r in enumerate(rows):
            inv_ref[pl.ds(r, 1)] = inv[u]
            tt_ref[r] = (wide[u] * (inv[u] * SCALE)).astype(BF16)
        return 0

    lax.fori_loop(0, count // unroll, body, 0)


def build_tables(owners, room, codes_end, names_ref, row_ref, target, turned, place, codes, wants, ends, tab_i, tab_f):
    count, listed = row_ref.shape
    lane = lax.broadcasted_iota(I32, (128, 128), 1)
    line = lax.broadcasted_iota(I32, (128, 128), 0)
    lane_f = lane.astype(F32)
    lower = (lane < line).astype(F32).astype(BF16)

    def flip(x):
        turned[...] = jnp.zeros_like(turned)
        turned[0:count, 0:listed] = x
        return jnp.transpose(turned[...])

    number = lax.broadcasted_iota(I32, row_ref.shape, 0)
    names = flip(names_ref[...].astype(F32))
    code = flip((row_ref[...] * count + number).astype(F32))
    want = flip(target)
    per = 128 // listed
    blocks = count // per
    offset = jnp.zeros((1, 128), F32)
    ends[...] = jnp.zeros_like(ends)
    for r in range(blocks):
        def column(x):
            return jnp.concatenate(
                [x[0:listed, r * per + i : r * per + i + 1] for i in range(per)], axis=0
            )

        hit = (column(names) == lane_f)
        ones = hit.astype(F32)
        rank = jnp.dot(lower, ones.astype(BF16), preferred_element_type=F32) + offset
        where = jnp.sum(jnp.where(hit, rank + lane_f * room, 0.0), axis=1, keepdims=True)
        place[r] = jnp.broadcast_to(where, (128, 128))
        codes[r] = jnp.broadcast_to(column(code), (128, 128))
        wants[r] = jnp.broadcast_to(column(want), (128, 128))
        for i in range(per):
            at = (i + 1) * listed - 1
            upto = rank[at : at + 1] + ones[at : at + 1]
            start = offset if i == 0 else before
            ends[r * per + i : r * per + i + 1] = jnp.where(
                upto > start, jnp.minimum(upto - 1.0, float(room)), float(room)
            )
            before = upto
        offset = before
    turned[...] = jnp.transpose(ends[...])
    tab_i[...] = jnp.zeros_like(tab_i)
    tab_f[...] = jnp.zeros_like(tab_f)
    mark = lax.broadcasted_iota(I32, (1, 128), 1)

    def one_owner(o, _):
        slot = lane_f + (o * room).astype(F32)
        sum_c = jnp.zeros((128, 128), F32)
        sum_w = jnp.zeros((128, 128), F32)
        for r in range(blocks):
            here = place[r] == slot
            sum_c = sum_c + jnp.where(here, codes[r], 0.0)
            sum_w = sum_w + jnp.where(here, wants[r], 0.0)
        c = jnp.clip(jnp.sum(sum_c, axis=0, keepdims=True).astype(I32), 0, codes_end - 1)
        whose = c & (count - 1)
        same = (whose == pltpu.roll(whose, 1, 1)) & (mark > 0)
        tab_i[o, 0:1] = c
        tab_i[o, 1:2] = jnp.clip(turned[pl.ds(o, 1)].astype(I32), 0, room)
        tab_f[o, 0:1] = jnp.sum(sum_w, axis=0, keepdims=True)
        tab_f[o, 1:2] = jnp.where(same, 1.0, 0.0)
        return 0

    lax.fori_loop(0, owners, one_owner, 0)


def negatives(first_step, last_step, unroll, rows_ref, each, tt_ref, qt_ref, acc_ref, sum_ref):
    width = qt_ref.shape[1]
    lane = lax.broadcasted_iota(I32, (1, width), 1)
    steps = each // unroll

    def body(b, _):
        holder, first = b // steps, lax.rem(b, steps) * unroll
        flipped = [tt_ref[rows_ref[holder, 0, first + u]] for u in range(unroll)]
        tiles = jnp.concatenate([jnp.transpose(t) for t in flipped], axis=0)
        sims = jnp.dot(tiles, qt_ref[...], preferred_element_type=F32)
        expo = jnp.exp2(sims)
        parts = [expo[u * 128 : (u + 1) * 128] for u in range(unroll)]
        logs = jnp.log2(
            jnp.concatenate([jnp.sum(x, axis=0, keepdims=True) for x in parts], axis=0)
        )
        top = jnp.exp2(lane_sum_of_groups(logs, 32, lane, width) * 0.1)
        factor = top * jnp.exp2(-logs)
        weights = jnp.concatenate(
            [(parts[u] * factor[u : u + 1]).astype(BF16) for u in range(unroll)], axis=0
        )
        acc_ref[...] += jnp.dot(
            jnp.concatenate(flipped, axis=1), weights, preferred_element_type=F32
        )
        sum_ref[0:1] += jnp.sum(top, axis=0, keepdims=True)
        return 0

    lax.fori_loop(first_step, last_step, body, 0)


def paired_dots(left, right):
    zero = jnp.zeros(left[0].shape, left[0].dtype)
    m = left[0].shape[0]
    out = []
    for i in range(0, len(left), 2):
        both = jnp.concatenate(
            [
                jnp.concatenate([left[i], zero], axis=1),
                jnp.concatenate([zero, left[i + 1]], axis=1),
            ],
            axis=0,
        )
        stacked = jnp.concatenate([right[i], right[i + 1]], axis=0)
        two = jnp.dot(both, stacked, preferred_element_type=F32)
        out += [two[:m], two[m:]]
    return out


def listed_pairs(src, room, unroll, group, tab_i, tab_f, w_ref, inv_ref, tt_ref, q_ref, pa, pb, p1, p2):
    zero = jnp.zeros((32, 128), F32)
    one = jnp.zeros((1, 1), F32)

    def body(b, carry):
        acc_a, acc_b, acc_1, acc_2 = carry
        ks = [b * unroll + u for u in range(unroll)]
        cs = [tab_i[src, 0, k] for k in ks]
        sims, expo, totals, weights, back, score, top, flat = [{} for _ in range(8)]
        steps = unroll // group
        for t in range(steps + 3):
            us = range(t * group, (t + 1) * group)
            if t < steps:
                dots = paired_dots([q_ref[cs[u] & 15] for u in us], [tt_ref[cs[u] >> 4] for u in us])
                sims.update(zip(us, dots))
            us = range((t - 1) * group, t * group)
            if 0 <= t - 1 < steps:
                for u in us:
                    expo[u] = jnp.exp2(sims.pop(u))
                    totals[u] = jnp.sum(expo[u], axis=-1, keepdims=True)
                for u in us:
                    weights[u] = (expo.pop(u) * inv_ref[pl.ds(cs[u] >> 4, 1)]).astype(BF16)
            us = range((t - 2) * group, (t - 1) * group)
            if 0 <= t - 2 < steps:
                dots = paired_dots([weights.pop(u) for u in us], [w_ref[cs[u] >> 4] for u in us])
                back.update(zip(us, dots))
                logs = {u: jnp.log2(totals.pop(u)) for u in us}
                for u in us:
                    flat[u] = jnp.exp2(-logs[u])
                for u in us:
                    score[u] = jnp.sum(logs[u], axis=0, keepdims=True) * 0.1
                for u in us:
                    top[u] = jnp.exp2(score[u])
            us = range((t - 3) * group, (t - 2) * group)
            if 0 <= t - 3 < steps:
                for u in us:
                    k = ks[u]
                    here = back.pop(u) * flat.pop(u)
                    target, stay = tab_f[src, 0, k], tab_f[src, 1, k]
                    acc_a = acc_a * stay + here * top[u]
                    acc_b = acc_b * stay + here * target
                    acc_1 = acc_1 * stay + top[u]
                    acc_2 = acc_2 * stay + score[u] * target
                    pa[k] = acc_a.astype(BF16)
                    pb[k] = acc_b.astype(BF16)
                    p1[pl.ds(k, 1)] = jnp.broadcast_to(acc_1, (1, 128))
                    p2[pl.ds(k, 1)] = jnp.broadcast_to(acc_2, (1, 128))
        return acc_a, acc_b, acc_1, acc_2

    lax.fori_loop(0, room // unroll, body, (zero, zero, one, one))


def kernel(
    owners, holders, room, chunks, sampled,
    names_ref, row_ref, neg_ref, teacher_ref, q_ref, index_ref,
    grad_ref, loss_ref,
    w, tt, inv, qall, qcur, qt, pa, pb, p1, p2, acc, nsum, flat_a, flat_s, stats,
    turned, ends, place, codes, wants, tab_i, tab_f, all_i, all_f, all_n, neg_own,
    back_buf, sum_buf, got, got_sum,
    code_s, mark_s, rows_s,
    load_sem, q_send, q_recv, i_send, i_recv, f_send, f_recv, n_send, n_recv,
    b_send, b_recv, s_send, s_recv, smem_sem,
):
    me = lax.axis_index("corpus")
    seat = lax.axis_index("blk")
    count, tokens = qcur.shape[0], qcur.shape[1]
    part = w.shape[0] // chunks
    barrier = pltpu.get_barrier_semaphore()

    def each(first, last, act):
        def body(k, _):
            act(k)
            return 0

        lax.fori_loop(first, last, body, 0)

    def loads(j):
        rows = pl.ds(j * part, part)
        return pltpu.make_async_copy(index_ref.at[rows], w.at[rows], load_sem.at[j])

    side = math.isqrt(owners)
    own = side // 2

    def shifted(m, sign):
        dy = side // 2 + lax.rem(m, side)
        dz = dy + m // side
        y = lax.rem(me // side + sign * lax.rem(dy, side) + side, side)
        z = lax.rem(lax.rem(me, side) + sign * lax.rem(dz, side) + side, side)
        return y * side + z

    def owner(m):
        return {"corpus": shifted(m, 1)}

    def peers(act):
        each(0, own, act)
        each(own + 1, owners, act)

    def holder(k):
        return {"blk": lax.rem(seat + k, holders)}

    def remote(src, dst, send, recv, k, device):
        return pltpu.make_async_remote_copy(
            src_ref=src, dst_ref=dst, send_sem=send.at[k], recv_sem=recv.at[k],
            device_id=device, device_id_type=MESH,
        )

    def greet(device):
        pl.semaphore_signal(barrier, inc=1, device_id=device, device_id_type=MESH)

    each(0, chunks, lambda j: loads(j).start())
    peers(lambda k: greet(owner(k)))
    each(1, holders, lambda k: greet(holder(k)))

    wide = q_ref[...].astype(F32)
    radius = jnp.sqrt(jnp.sum(wide * wide, axis=-1, keepdims=True) + EPS)
    rounded = (wide / radius).astype(BF16)
    qall[me] = rounded.reshape(qcur.shape)
    qt[...] = jnp.transpose(rounded)
    neg_own[...] = jnp.zeros_like(neg_own)
    neg_own[0:1, 0:sampled] = neg_ref[...]
    all_n[seat] = neg_own[...]

    pl.semaphore_wait(barrier, owners + holders - 2)

    def n_copy(k):
        return remote(neg_own, all_n.at[seat], n_send, n_recv, k, holder(k))

    def q_copy(k):
        return remote(qall.at[me], qall.at[me], q_send, q_recv, k, owner(k))

    def table_copies(k):
        to = shifted(k, 1)
        return (
            remote(tab_i.at[to], all_i.at[me], i_send, i_recv, k, owner(k)),
            remote(tab_f.at[to], all_f.at[me], f_send, f_recv, k, owner(k)),
        )

    each(1, holders, lambda k: n_copy(k).start())
    at_once = 4
    each(0, own, lambda k: q_copy(k).start())
    each(own + 1, at_once, lambda k: q_copy(k).start())

    teacher = teacher_ref[...]
    log_target = teacher - jnp.log(jnp.sum(jnp.exp(teacher), axis=1, keepdims=True))
    target = jnp.exp(log_target)
    stats[0] = jnp.broadcast_to(jnp.sum(target * log_target, axis=1, keepdims=True), (count, 128))
    stats[1] = jnp.broadcast_to(jnp.sum(target, axis=1, keepdims=True), (count, 128))
    build_tables(
        owners, room, w.shape[0] * count, names_ref, row_ref, target, turned, place, codes, wants, ends, tab_i, tab_f
    )
    all_i[me] = tab_i[me]
    all_f[me] = tab_f[me]
    peers(lambda k: [copy.start() for copy in table_copies(k)])

    def prepare(j):
        @pl.when(j < owners - at_once)
        def _():
            q_copy(at_once + j).start()

        loads(j).wait()
        transpose_pass(j * part, part, 8, w, inv, tt)

    each(0, chunks, prepare)
    each(1, holders, lambda k: n_copy(k).wait())
    peers(lambda k: [copy.wait() for copy in table_copies(k)])
    moves = [
        pltpu.make_async_copy(all_n, rows_s, smem_sem.at[0]),
        pltpu.make_async_copy(all_i, code_s, smem_sem.at[1]),
        pltpu.make_async_copy(all_f, mark_s, smem_sem.at[2]),
    ]
    for move in moves:
        move.start()
    for move in moves:
        move.wait()
    acc[...] = jnp.zeros_like(acc)
    nsum[...] = jnp.zeros_like(nsum)
    neg_steps = holders * sampled // 12
    early = 0
    negatives(0, early, 12, rows_s, sampled, tt, qt, acc, nsum)

    pa[room] = jnp.zeros((tokens, 128), BF16)
    pb[room] = jnp.zeros((tokens, 128), BF16)
    p1[room : room + 8] = jnp.zeros((8, 128), F32)
    p2[room : room + 8] = jnp.zeros((8, 128), F32)

    def back_copies(k):
        to = {"corpus": shifted(k, -1)}
        return (
            remote(back_buf.at[k], got.at[k], b_send, b_recv, k, to),
            remote(sum_buf.at[k], got_sum.at[k], s_send, s_recv, k, to),
        )

    def source(k):
        src = shifted(k, -1)

        @pl.when(k != own)
        def _():
            q_copy(k).wait_recv()

        qcur[...] = qall[src]
        listed_pairs(src, room, 64, 8, code_s, mark_s, w, inv, tt, qcur, pa, pb, p1, p2)

        def extract(q, _):
            at = code_s[src, 1, q]
            back_buf[k, q, 0:tokens] = pa[at]
            back_buf[k, q, tokens : 2 * tokens] = pb[at]
            sum_buf[k, 0, pl.ds(q, 1)] = p1[pl.ds(at, 1)]
            sum_buf[k, 1, pl.ds(q, 1)] = p2[pl.ds(at, 1)]
            return 0

        lax.fori_loop(0, count, extract, 0, unroll=4)

        @pl.when(k != own)
        def _():
            for copy in back_copies(k):
                copy.start()

    each(0, owners, source)
    negatives(early, neg_steps, 12, rows_s, sampled, tt, qt, acc, nsum)

    turned_a = jnp.transpose(acc[...]) * (1.0 / SCALE)
    turned_s = jnp.transpose(jnp.broadcast_to(nsum[0:1], (128, count * tokens)))
    flat_a[...] = turned_a.reshape(flat_a.shape)
    flat_s[...] = turned_s.reshape(flat_s.shape)

    peers(lambda k: [copy.wait() for copy in back_copies(k)])
    peers(lambda k: q_copy(k).wait_send())
    sums = sum_buf[own]
    others = [k for k in range(owners) if k != own]
    for k in others:
        sums = sums + got_sum[k]
    p1[0:count] = sums[0]
    p2[0:count] = sums[1]

    def finish(q, _):
        part_a = flat_a[q] + back_buf[own, q, 0:tokens].astype(F32)
        part_b = back_buf[own, q, tokens : 2 * tokens].astype(F32)
        for k in others:
            part_a = part_a + got[k, q, 0:tokens].astype(F32)
            part_b = part_b + got[k, q, tokens : 2 * tokens].astype(F32)
        whole = flat_s[q] + p1[pl.ds(q, 1)]
        pulled = part_a / whole - part_b
        raw = q_ref[pl.ds(pl.multiple_of(q * tokens, tokens), tokens)].astype(F32)
        rad = jnp.sqrt(jnp.sum(raw * raw, axis=-1, keepdims=True) + EPS)
        unit = raw / rad
        along = jnp.sum(unit * pulled, axis=-1, keepdims=True)
        grad_ref[q] = (pulled - unit * along) / rad
        one = pl.ds(q, 1)
        stats[2, one] = stats[0, one] - LN2 * p2[one] + jnp.log(whole[0:1]) * stats[1, one]
        return 0

    lax.fori_loop(0, count, finish, 0, unroll=2)
    turned[...] = jnp.zeros_like(turned)
    turned[0:count] = stats[2]
    loss_ref[...] = jnp.transpose(turned[...])[0:1, 0:count]


def step(queries, index, cand_owner, cand_row, neg_row, teacher):
    count, tokens, dim = queries.shape
    listed = cand_row.shape[1]
    owners, holders = lax.axis_size("corpus"), lax.axis_size("blk")
    room = 2 * count * listed // owners
    passages = index.shape[0]
    width = count * tokens
    smem = pltpu.SMEM
    vmem = pl.BlockSpec(memory_space=pltpu.VMEM)
    dma = pltpu.SemaphoreType.DMA
    chunks = 16
    grads, losses = pl.pallas_call(
        functools.partial(kernel, owners, holders, room, chunks, neg_row.shape[1]),
        out_shape=[
            jax.ShapeDtypeStruct((count, tokens, dim), F32),
            jax.ShapeDtypeStruct((1, count), F32),
        ],
        in_specs=[vmem] * 5 + [pl.BlockSpec(memory_space=pl.ANY)],
        out_specs=[vmem, vmem],
        scratch_shapes=[
            pltpu.VMEM(index.shape, BF16),
            pltpu.VMEM((passages, dim, index.shape[1]), BF16),
            pltpu.VMEM((passages, 128), F32),
            pltpu.VMEM((owners, count, tokens, dim), BF16),
            pltpu.VMEM((count, tokens, dim), BF16),
            pltpu.VMEM((dim, width), BF16),
            pltpu.VMEM((room + 1, tokens, dim), BF16),
            pltpu.VMEM((room + 1, tokens, dim), BF16),
            pltpu.VMEM((room + 8, 128), F32),
            pltpu.VMEM((room + 8, 128), F32),
            pltpu.VMEM((dim, width), F32),
            pltpu.VMEM((8, width), F32),
            pltpu.VMEM((count, tokens, dim), F32),
            pltpu.VMEM((count, tokens, dim), F32),
            pltpu.VMEM((3, count, 128), F32),
            pltpu.VMEM((128, 128), F32),
            pltpu.VMEM((128, 128), F32),
            pltpu.VMEM((count * listed // 128, 128, 128), F32),
            pltpu.VMEM((count * listed // 128, 128, 128), F32),
            pltpu.VMEM((count * listed // 128, 128, 128), F32),
            pltpu.VMEM((owners, 8, 128), I32),
            pltpu.VMEM((owners, 8, 128), F32),
            pltpu.VMEM((owners, 8, 128), I32),
            pltpu.VMEM((owners, 8, 128), F32),
            pltpu.VMEM((holders, 8, 128), I32),
            pltpu.VMEM((8, 128), I32),
            pltpu.VMEM((owners, count, 2 * tokens, dim), BF16),
            pltpu.VMEM((owners, 2, count, 128), F32),
            pltpu.VMEM((owners, count, 2 * tokens, dim), BF16),
            pltpu.VMEM((owners, 2, count, 128), F32),
            smem((owners, 8, 128), I32),
            smem((owners, 8, 128), F32),
            smem((holders, 8, 128), I32),
            dma((chunks,)),
            *[dma((owners,)) for _ in range(6)],
            *[dma((holders,)) for _ in range(2)],
            *[dma((owners,)) for _ in range(4)],
            dma((3,)),
        ],
        compiler_params=pltpu.CompilerParams(
            collective_id=0, has_side_effects=True, vmem_limit_bytes=60 << 20
        ),
        name="distill",
    )(
        cand_owner.reshape(count, listed), cand_row, neg_row, teacher,
        queries.reshape(width, dim), index,
    )
    return losses.reshape(count), grads


def solution(mesh):
    both = ("corpus", "blk")
    return jax.shard_map(
        step,
        mesh=mesh,
        in_specs=(
            P(both, None, None), P("corpus", None, None), P(both, None, None),
            P(both, None), P(both, None), P(both, None),
        ),
        out_specs=(P(both), P(both, None, None)),
        check_vma=False,
    )
```
